128 devices in a mesh: dp: 8 (over z_hi, y), fsdp: 16 (over z_lo, x, core).
Axes of the slice: x: 4, y: 4, z: 4 (z_hi: 2, z_lo: 2; z = z_hi * 2 + z_lo), core: 2. Of those that a mesh axis runs over, the one named last changes fastest.
Arguments:
- weight: float32 [4096, 15360], P('fsdp', 'dp'), may hold values from -0.09375 to 0.09375
- history: float32 [7, 4096, 15360], P(None, 'fsdp', 'dp'), may hold values from -6 to 6
- newest: int32 [1], replicated, may hold values from 0 to 6
- band: float32 [8], replicated, may hold values from 0.5 to 1.5
- fresh: bfloat16 [4096, 15360], P('fsdp', 'dp'), may hold values from -6 to 6
- x_grad: bfloat16 [1024, 4096], P('dp', 'fsdp'), may hold values from -96 to 96
- dy_grad: bfloat16 [1024, 15360], P('dp'), may hold values from -6 to 6
- x_next: bfloat16 [6144, 4096], P('fsdp'), may hold values from -6 to 6
Outputs:
- new_weight: float32 [4096, 15360], P('fsdp', 'dp')
- noise_now: float32 [4096, 15360], P('fsdp', 'dp')
- next_out: bfloat16 [6144, 15360], P('fsdp', 'dp')
The draws below stay inside these ranges and needn't reach their ends.
All inputs are finite; a program needn't handle non-finite values.
Results may differ from the reference program's by a relative error of at most 0.005.
Values may be sent and summed in bfloat16 or wider, within the bound.
A program may use at most 128 MiB of HBM per device.

```python
import math
import jax
import jax.numpy as jnp
from jax import lax

D = 4096
F = 15360
BAND = 8
SLOTS = 7
TOKENS = 1024
NEXT_TOKENS = 6144


def draw_x_grad(key, part):
    first_key, second_key = jax.random.split(jax.random.fold_in(key, 11))
    row_scale = jnp.exp(jax.random.uniform(first_key, (TOKENS, 1), jnp.float32, jnp.log(0.3), jnp.log(3.0)))
    column_ramp = 1.0 + 2.0 * jnp.arange(D, dtype=jnp.float32)[None, :] / (D - 1)
    values = jnp.clip(jax.random.normal(second_key, (TOKENS, D), jnp.float32), -4.0, 4.0)
    return (values * row_scale * column_ramp).astype(jnp.bfloat16)


def raised(values, rng, source, target, shards_of, factor):
    def block_of(position):
        return (jnp.arange(values.shape[position]) // (values.shape[position] // shards_of)).reshape((-1,) + (1,) * (values.ndim - 1 - position))

    near = jax.random.permutation(rng, shards_of)[block_of(target)]
    second = (block_of(target) + shards_of // 2) % shards_of
    return jnp.where((block_of(source) == near) | (block_of(source) == second), factor * values, values)


def level_of(rng, extent, cuts, smallest, high):
    def one(position, parts):
        steps = jax.random.uniform(jax.random.fold_in(jax.random.fold_in(rng, 6), position), (parts,), jnp.float32, smallest / len(cuts), high / len(cuts))
        return jnp.repeat(jnp.exp(steps), extent[position] // parts).reshape((-1,) + (1,) * (len(extent) - position - 1))

    loudness = one(*cuts[0])
    for cut in cuts[1:]:
        loudness = loudness * one(*cut)
    return loudness


def centred(stream_key, shape, deviation, bound, cuts=(), kind=jnp.bfloat16):
    gain = level_of(stream_key, shape, cuts, -0.22, 0.18) if cuts else 1.0
    array = jax.random.normal(stream_key, shape, jnp.float32) * deviation * gain
    return jnp.minimum(jnp.maximum(array, -bound), bound).astype(kind)


def heavy_noise(rng, dims, scale, limit, pieces, heavy, held_as=jnp.bfloat16):
    drawn = scale * jax.random.normal(rng, dims, jnp.float32)
    if pieces:
        drawn = drawn * level_of(rng, dims, pieces, -0.22, 0.18)
    return jnp.clip(raised(drawn, jax.random.fold_in(rng, 3), *heavy), -limit, limit).astype(held_as)


def setup_inputs(seed: int = 0) -> dict:
    splits = jax.random.split(jax.random.key(seed), 9)
    return {
        "weight": centred(splits[0], (D, F), D ** -0.5, 0.09375, ((0, 16), (1, 8)), jnp.float32),
        "history": centred(splits[1], (SLOTS, D, F), 1.0, 6.0, ((1, 16), (2, 8)), jnp.float32),
        "newest": jax.random.randint(splits[2], (1,), 0, SLOTS).astype(jnp.int32),
        "band": jnp.clip(jax.random.uniform(splits[3], (BAND,), jnp.float32, 0.5, 1.5), 0.5, 1.5),
        "fresh": centred(splits[4], (D, F), 1.0, 6.0, ((0, 16), (1, 8))),
        "x_grad": draw_x_grad(jax.random.fold_in(splits[8], 71), 0),
        "dy_grad": heavy_noise(splits[6], (TOKENS, F), 1.0, 6.0, ((0, 8),), (0, 1, 8, 2.0)),
        "x_next": centred(splits[7], (NEXT_TOKENS, D), 1.0, 6.0, ((0, 16),)),
    }


eps_value = 1e-06
learn_rate = 0.2
noise_multiplier = 0.01

def slot_weights(newest, band, slots):
    slot_index = jnp.arange(slots, dtype=jnp.int32)
    ages = (newest[0] - slot_index) % slots + 1
    table_index = jnp.arange(slots + 1, dtype=jnp.int32)
    return lax.optimization_barrier(jnp.sum(jnp.where(ages[:, None] == table_index[None, :], band[None, :], 0.0), axis=1))

def reference(weight, history, newest, band, fresh, x_grad, dy_grad, x_next):
    clip_bound = 2.0 * math.sqrt(D * F)
    x_float = x_grad.astype(jnp.float32)
    feature_sq = lax.optimization_barrier(jnp.sum(x_float * x_float, axis=1))
    output_sq = lax.optimization_barrier(jnp.sum(jnp.square(dy_grad.astype(jnp.float32)), axis=1))
    factor = jnp.minimum(1.0, clip_bound / jnp.sqrt(feature_sq * output_sq + eps_value))
    clipped = (factor[:, None] * x_float).astype(jnp.bfloat16)
    contract = (((0,), (0,)), ((), ()))
    gradient = lax.dot_general(clipped, dy_grad, contract, preferred_element_type=jnp.float32)
    mixing = slot_weights(newest, band, SLOTS)
    combined = jnp.tensordot(mixing, history, axes=1, precision=lax.Precision.HIGHEST)
    noise_now = (fresh.astype(jnp.float32) - combined) / band[0]
    new_weight = weight - learn_rate * (gradient + noise_multiplier * clip_bound * noise_now) / TOKENS
    weight_half = new_weight.astype(jnp.bfloat16)
    next_out = jnp.dot(x_next, weight_half, preferred_element_type=jnp.float32).astype(jnp.bfloat16)
    return (new_weight, noise_now, next_out)
```

```python
import math

import jax
import jax.numpy as jnp
from jax import lax
from jax.sharding import PartitionSpec as P

eps_value = 1e-06
learn_rate = 0.2
noise_multiplier = 0.01


def slot_weights(newest, band, slots):
    slot_index = jnp.arange(slots, dtype=jnp.int32)
    ages = (newest[0] - slot_index) % slots + 1
    table_index = jnp.arange(slots + 1, dtype=jnp.int32)
    return jnp.sum(jnp.where(ages[:, None] == table_index[None, :], band[None, :], 0.0), axis=1)


def local(weight, history, newest, band, fresh, x_grad, dy_grad, x_next):
    full_width = x_next.shape[1]
    hidden_units = dy_grad.shape[1]
    clip_bound = 2.0 * math.sqrt(full_width * hidden_units)
    dy_mine = lax.all_to_all(dy_grad, "dp", split_axis=1, concat_axis=0, tiled=True)
    x_float = x_grad.astype(jnp.float32)
    feature_sq = lax.psum(jnp.sum(x_float * x_float, axis=1), "fsdp")
    output_sq = jnp.sum(jnp.square(dy_grad.astype(jnp.float32)), axis=1)
    factor = jnp.minimum(1.0, clip_bound / jnp.sqrt(feature_sq * output_sq + eps_value))
    clipped = (factor[:, None] * x_float).astype(jnp.bfloat16)
    clipped_all = lax.all_gather(clipped, "dp", axis=0, tiled=True)
    contract = (((0,), (0,)), ((), ()))
    gradient = lax.dot_general(clipped_all, dy_mine, contract, preferred_element_type=jnp.float32)
    tokens_all = x_grad.shape[0] * lax.axis_size("dp")
    slots = history.shape[0]
    mixing = slot_weights(newest, band, slots)
    combined = jnp.tensordot(mixing, history, axes=1, precision=lax.Precision.HIGHEST)
    noise_now = (fresh.astype(jnp.float32) - combined) / band[0]
    new_weight = (
        weight - learn_rate * (gradient + noise_multiplier * clip_bound * noise_now) / tokens_all
    )
    weight_half = new_weight.astype(jnp.bfloat16)
    next_float = jnp.dot(
        x_next,
        lax.all_gather(weight_half, "fsdp", axis=0, tiled=True),
        preferred_element_type=jnp.float32,
    )
    return (new_weight, noise_now, next_float.astype(jnp.bfloat16))


def solution(mesh):
    in_specs = (
        P("fsdp", "dp"),
        P(None, "fsdp", "dp"),
        P(),
        P(),
        P("fsdp", "dp"),
        P("dp", "fsdp"),
        P("dp", None),
        P("fsdp", None),
    )
    out_specs = (P("fsdp", "dp"), P("fsdp", "dp"), P("fsdp", "dp"))
    return jax.shard_map(local, mesh=mesh, in_specs=in_specs, out_specs=out_specs, check_vma=False)
```

```python
import functools
import math

import jax
import jax.numpy as jnp
from jax import lax
from jax.experimental import pallas as pl
from jax.experimental.pallas import tpu as pltpu
from jax.sharding import PartitionSpec as P

eps_value = 1e-06
learn_rate = 0.2
noise_multiplier = 0.01

LANES = 128
ROWS_IN = 224
PIECES = 4
LAG_B, LAG_C, LAG_D, LAG_E, LAG_F = 1, 3, 4, 6, 8
EARLY = 5
MESH = pl.DeviceIdType.MESH


def wait_for(ref, sem):
    pltpu.make_async_copy(ref, ref, sem).wait()


def kernel(
    clip_bound, tokens_all,
    newest, band, weight, history, fresh, x_grad, dy_grad, x_next,
    new_weight, noise_now, next_out,
    hist, wv, fr, dyb, wb, xo, xp, psend, precv, own, obuf, xg, dyq, cts, sbuf, rbuf,
    s_hist, s_wv, s_fr, s_dyr, s_dyf, s_left, s_right, s_opp, s_sib, s_part, s_stat_s, s_stat_r, s_misc,
):
    chunks = hist.shape[0]
    slots = hist.shape[1]
    half = xo.shape[1]
    units = chunks * LANES
    d, f = lax.axis_index("dp"), lax.axis_index("fsdp")
    hi, y = d // 4, d % 4
    lo, x, c = f // 8, (f // 2) % 4, f % 2
    oc = 1 - c
    xr, xl, xx = (x + 1) % 4, (x + 3) % 4, (x + 2) % 4

    def at(lo_, x_, c_):
        return (d, lo_ * 8 + x_ * 2 + c_)

    sibling = at(lo, x, oc)
    right, left = at(lo, xr, c), at(lo, xl, c)
    inner = at(1 - lo, x, c)
    flipped = (1 - lo) * 8 + x * 2 + c
    outer = ((1 - hi) * 4 + y, flipped)
    same_hi = [(hi * 4 + (y + s) % 4, f) for s in (1, 3, 2)]
    other_hi = [((1 - hi) * 4 + (y + s) % 4, flipped) for s in (0, 1, 3, 2)]
    other_hi_same_f = [((1 - hi) * 4 + (y + s) % 4, f) for s in (0, 1, 3, 2)]

    (S_XG, S_DYQ, S_XO, S_XIN, S_XOUT, S_CT, S_DYS, S_DYFS, S_W1, S_W2, S_W3, S_PS, S_XS1, S_XS2, S_CTS,
     S_ONW, S_ONN, S_OUT) = range(18)

    def cols(k):
        return pl.ds(pl.multiple_of(k * LANES, LANES), LANES)

    def remote(src, dst, send, recv, to):
        pltpu.make_async_remote_copy(src, dst, send, recv, device_id=to, device_id_type=MESH).start()

    barrier = pltpu.get_barrier_semaphore()
    peers = [sibling, right, left, inner] + same_hi + other_hi_same_f + other_hi
    for peer in peers:
        pl.semaphore_signal(barrier, inc=1, device_id=peer, device_id_type=MESH)

    share = f // 2
    pltpu.make_async_copy(x_grad, xg, s_misc.at[S_XG]).start()
    pltpu.make_async_copy(
        dy_grad.at[:, pl.ds(pl.multiple_of(share * units, LANES), units)], dyq, s_misc.at[S_DYQ]
    ).start()

    def fetch(k):
        pltpu.make_async_copy(history.at[:, :, cols(k)], hist.at[k], s_hist.at[k]).start()
        pltpu.make_async_copy(weight.at[:, cols(k)], wv.at[k], s_wv.at[k]).start()
        pltpu.make_async_copy(fresh.at[:, cols(k)], fr.at[k], s_fr.at[k]).start()

    my_rows = pl.ds(pl.multiple_of(c * 64, 64), 64)

    def fetch_dy(k):
        column = pl.ds(pl.multiple_of(d * units + k * LANES, LANES), LANES)
        pltpu.make_async_copy(dy_grad.at[my_rows, column], dyb.at[k, d, c], s_dyr.at[k]).start()

    @pl.loop(0, 2)
    def _(k):
        fetch_dy(k)
        fetch(k)

    wait_for(xg, s_misc.at[S_XG])
    x_t = xg[...].astype(jnp.float32).T
    feature_part = jnp.sum(x_t * x_t, axis=0, keepdims=True)
    wait_for(dyq, s_misc.at[S_DYQ])
    total = jnp.zeros((LANES, LANES), jnp.float32)
    for n in range(chunks):
        piece = dyq[:, n * LANES : (n + 1) * LANES].astype(jnp.float32)
        total = total + piece * piece
    output_part = 0.5 * jnp.sum(total.T, axis=0, keepdims=True)
    row = lax.broadcasted_iota(jnp.int32, (8, LANES), 0)
    sbuf[0] = jnp.where(row == 0, feature_part, jnp.where(row == 1, output_part, 0.0))

    pl.semaphore_wait(barrier, len(peers))

    def stat_send(r, to):
        remote(sbuf.at[r], rbuf.at[r], s_stat_s.at[r], s_stat_r.at[r], to)

    def stat_take(r):
        wait_for(rbuf.at[r], s_stat_r.at[r])
        sbuf[r + 1] = sbuf[r] + rbuf[r]

    def send_dy_to(k, to):
        column = pl.ds(pl.multiple_of(to[0] * units + k * LANES, LANES), LANES)
        remote(dy_grad.at[my_rows, column], dyb.at[k, d, c], s_misc.at[S_DYS], s_dyr.at[k], to)

    def send_dy(k):
        for to in other_hi + same_hi:
            send_dy_to(k, to)

    stat_send(0, sibling)
    send_dy(0)
    stat_take(0)
    stat_send(1, at(lo, x + 1 - 2 * (x % 2), c))
    other_half = pl.multiple_of((1 - lo) * half, LANES)
    remote(
        x_next.at[0:ROWS_IN, pl.ds(other_half, half)], xp.at[0:ROWS_IN], s_misc.at[S_XS1], s_misc.at[S_XIN], inner
    )
    send_dy(1)
    stat_take(1)
    stat_send(2, at(lo, 3 - x, c))
    width = half // PIECES

    def send_piece(q):
        remote(
            x_next.at[ROWS_IN:, pl.ds(pl.multiple_of(other_half + q * width, LANES), width)],
            xp.at[ROWS_IN:, pl.ds(pl.multiple_of(q * width, LANES), width)],
            s_misc.at[S_XS2], s_misc.at[S_XOUT], outer,
        )

    stat_take(2)
    stat_send(3, inner)

    @pl.loop(2, EARLY)
    def _(k):
        send_dy(k)
        send_piece(k - 2)

    stat_take(3)
    both = sbuf[4]
    factor = jnp.minimum(1.0, clip_bound / jnp.sqrt(both[0:1] * both[1:2] + eps_value))
    mine = pl.ds(pl.multiple_of(d * LANES, LANES), LANES)
    cts[:, mine] = (x_t * factor).astype(jnp.bfloat16)
    for to in other_hi_same_f + same_hi:
        remote(cts.at[:, mine], cts.at[:, mine], s_misc.at[S_CTS], s_misc.at[S_CT], to)

    for q in range(EARLY - 2, PIECES):
        send_piece(q)

    @pl.loop(EARLY, chunks)
    def _(k):
        send_dy(k)

    pltpu.make_async_copy(x_next.at[:, pl.ds(pl.multiple_of(lo * half, LANES), half)], xo, s_misc.at[S_XO]).start()

    @pl.loop(2, chunks)
    def _(k):
        fetch_dy(k)
        fetch(k)

    first = newest[0]
    mixing = [band[lax.rem(first + (slots - s), slots) + 1] for s in range(slots)]
    now_coefficient = band[0]

    wait_for(cts.at[:, 0 : 7 * LANES], s_misc.at[S_CT])

    def stage_a(k):
        wait_for(dyb.at[k, :, c], s_dyr.at[k])
        remote(dyb.at[k, :, c], dyb.at[k, :, c], s_misc.at[S_DYFS], s_dyf.at[k], sibling)

    def stage_b(k):
        wait_for(hist.at[k], s_hist.at[k])
        wait_for(wv.at[k], s_wv.at[k])
        wait_for(fr.at[k], s_fr.at[k])
        combined = mixing[0] * hist[k, 0]
        for s in range(1, slots):
            combined = combined + mixing[s] * hist[k, s]
        noise = (fr[k].astype(jnp.float32) - combined) / jnp.full(combined.shape, now_coefficient, jnp.float32)
        hist[k, 0] = noise
        wait_for(dyb.at[k, :, oc], s_dyf.at[k])
        gradient = jnp.dot(cts[...], dyb[k].reshape(8 * LANES, LANES), preferred_element_type=jnp.float32)
        updated = wv[k] - learn_rate * (gradient + (noise_multiplier * clip_bound) * noise) * (1.0 / tokens_all)
        wb[k, x, c] = updated.astype(jnp.bfloat16)
        wv[k] = updated
        block = wb.at[k, x, c]
        remote(block, block, s_misc.at[S_W1], s_left.at[k], right)
        remote(block, block, s_misc.at[S_W1], s_right.at[k], left)
        remote(block, block, s_misc.at[S_W1], s_sib.at[k], sibling)
        pltpu.make_async_copy(hist.at[k, 0], noise_now.at[:, cols(k)], s_misc.at[S_ONN]).start()
        pltpu.make_async_copy(wv.at[k], new_weight.at[:, cols(k)], s_misc.at[S_ONW]).start()

    upper, lower = pl.ds(0, LANES), pl.ds(LANES, LANES)

    def stage_c(k):
        from_left, from_right = wb.at[k, xl, c], wb.at[k, xr, c]
        wait_for(from_left, s_left.at[k])
        top = wb.at[k, xl, c, upper]
        remote(top, top, s_misc.at[S_W2], s_opp.at[k], right)
        remote(from_left, from_left, s_misc.at[S_W3], s_sib.at[k], sibling)
        wait_for(from_right, s_right.at[k])
        bottom = wb.at[k, xr, c, lower]
        remote(bottom, bottom, s_misc.at[S_W2], s_opp.at[k], left)
        remote(from_right, from_right, s_misc.at[S_W3], s_sib.at[k], sibling)

    def stage_d(k):
        block = wb.at[k, xx, c]
        wait_for(block, s_opp.at[k])
        remote(block, block, s_misc.at[S_W3], s_sib.at[k], sibling)

    def multiply(ks):
        parts = [wb[k].reshape(half, LANES) for k in ks]
        rhs = parts[0] if len(ks) == 1 else jnp.concatenate(parts, axis=1)
        theirs = jnp.dot(xp[...], rhs, preferred_element_type=jnp.float32).astype(jnp.bfloat16)
        for n, k in enumerate(ks):
            psend[k] = theirs[:, n * LANES : (n + 1) * LANES]
            remote(psend.at[k], precv.at[k], s_misc.at[S_PS], s_part.at[k], inner)
        ours = jnp.dot(xo[...], rhs, preferred_element_type=jnp.float32)
        for n, k in enumerate(ks):
            own[k] = ours[:, n * LANES : (n + 1) * LANES]

    def stage_e(k):
        @pl.when(k == 0)
        def _():
            wait_for(xo, s_misc.at[S_XO])
            wait_for(xp.at[0:ROWS_IN], s_misc.at[S_XIN])
            wait_for(xp.at[ROWS_IN:], s_misc.at[S_XOUT])

        wait_for(wb.at[k, :, oc], s_sib.at[k])

        @pl.when(k % 2 == 1)
        def _():
            multiply((k - 1, k))

        if chunks % 2 == 1:

            @pl.when(k == chunks - 1)
            def _():
                multiply((k,))

    def stage_f(k):
        wait_for(precv.at[k], s_part.at[k])
        obuf[k] = (own[k] + precv[k].astype(jnp.float32)).astype(jnp.bfloat16)
        pltpu.make_async_copy(obuf.at[k], next_out.at[:, cols(k)], s_misc.at[S_OUT]).start()

    def staged(stage, t, lag):
        k = t - lag

        @pl.when((k >= 0) & (k < chunks))
        def _():
            stage(k)

    @pl.loop(0, chunks + LAG_F)
    def _(t):
        staged(stage_c, t, LAG_C)
        staged(stage_d, t, LAG_D)
        staged(stage_a, t, 0)
        staged(stage_b, t, LAG_B)
        staged(stage_e, t, LAG_E)
        staged(stage_f, t, LAG_F)

    for r in range(4):
        wait_for(sbuf.at[r], s_stat_s.at[r])
    wait_for(dyb.at[:, 0:7, 0], s_misc.at[S_DYS])
    wait_for(dyb.at[:, :, 0], s_misc.at[S_DYFS])
    wait_for(xp.at[0:ROWS_IN], s_misc.at[S_XS1])
    wait_for(xp.at[ROWS_IN:], s_misc.at[S_XS2])
    wait_for(cts.at[:, 0 : 7 * LANES], s_misc.at[S_CTS])
    wait_for(wb.at[:, 0:3, 0], s_misc.at[S_W1])
    wait_for(wb.at[:, 0, 0], s_misc.at[S_W2])
    wait_for(wb.at[:, 0:3, 0], s_misc.at[S_W3])
    wait_for(psend, s_misc.at[S_PS])
    wait_for(hist.at[:, 0], s_misc.at[S_ONN])
    wait_for(wv, s_misc.at[S_ONW])
    wait_for(obuf, s_misc.at[S_OUT])


def local(weight, history, newest, band, fresh, x_grad, dy_grad, x_next):
    slots, rows, units = history.shape
    tokens, full_width = x_next.shape
    hidden_units = dy_grad.shape[1]
    clip_bound = 2.0 * math.sqrt(full_width * hidden_units)
    tokens_all = x_grad.shape[0] * lax.axis_size("dp")
    chunks = units // LANES
    half = full_width // 2
    any_space = pl.BlockSpec(memory_space=pl.ANY)
    scalars = pl.BlockSpec(memory_space=pltpu.SMEM)
    f32, b16 = jnp.float32, jnp.bfloat16
    per_chunk = pltpu.SemaphoreType.DMA((chunks,))
    return pl.pallas_call(
        functools.partial(kernel, clip_bound, tokens_all),
        out_shape=(
            jax.ShapeDtypeStruct((rows, units), f32),
            jax.ShapeDtypeStruct((rows, units), f32),
            jax.ShapeDtypeStruct((tokens, units), b16),
        ),
        in_specs=[scalars, scalars] + [any_space] * 6,
        out_specs=(any_space,) * 3,
        scratch_shapes=[
            pltpu.VMEM((chunks, slots, rows, LANES), f32),
            pltpu.VMEM((chunks, rows, LANES), f32),
            pltpu.VMEM((chunks, rows, LANES), b16),
            pltpu.VMEM((chunks, 8, 2, 64, LANES), b16),
            pltpu.VMEM((chunks, 4, 2, rows, LANES), b16),
            pltpu.VMEM((tokens, half), b16),
            pltpu.VMEM((tokens, half), b16),
            pltpu.VMEM((chunks, tokens, LANES), b16),
            pltpu.VMEM((chunks, tokens, LANES), b16),
            pltpu.VMEM((chunks, tokens, LANES), f32),
            pltpu.VMEM((chunks, tokens, LANES), b16),
            pltpu.VMEM(x_grad.shape, b16),
            pltpu.VMEM((x_grad.shape[0], units), b16),
            pltpu.VMEM((rows, tokens_all), b16),
            pltpu.VMEM((5, 8, LANES), f32),
            pltpu.VMEM((4, 8, LANES), f32),
        ]
        + [per_chunk] * 10
        + [pltpu.SemaphoreType.DMA((4,)), pltpu.SemaphoreType.DMA((4,)), pltpu.SemaphoreType.DMA((18,))],
        compiler_params=pltpu.CompilerParams(
            collective_id=0, has_side_effects=True, vmem_limit_bytes=67043328
        ),
        name="step",
    )(newest, band, weight, history, fresh, x_grad, dy_grad, x_next)


def solution(mesh):
    in_specs = (
        P("fsdp", "dp"),
        P(None, "fsdp", "dp"),
        P(),
        P(),
        P("fsdp", "dp"),
        P("dp", "fsdp"),
        P("dp", None),
        P("fsdp", None),
    )
    out_specs = (P("fsdp", "dp"), P("fsdp", "dp"), P("fsdp", "dp"))
    return jax.shard_map(local, mesh=mesh, in_specs=in_specs, out_specs=out_specs, check_vma=False)
```

```python
import functools
import math

import jax
import jax.numpy as jnp
from jax import lax
from jax.experimental import pallas as pl
from jax.experimental.pallas import tpu as pltpu
from jax.sharding import PartitionSpec as P

eps_value = 1e-06
learn_rate = 0.2
noise_multiplier = 0.01

LANES = 128
ROWS_IN = 256
PIECES = 4
ROWS_FIRST = 64
LAG_B, LAG_C, LAG_D, LAG_E, LAG_F = 1, 3, 5, 7, 10
AHEAD = 5
SEMS = 24
MESH = pl.DeviceIdType.MESH


def wait_for(ref, sem):
    pltpu.make_async_copy(ref, ref, sem).wait()


def kernel(
    clip_bound, tokens_all,
    newest, band, weight, history, fresh, x_grad, dy_grad, x_next,
    new_weight, noise_now, next_out,
    hist, wv, fr, dyb, wb, xo, xp, psend, precv, own, obuf, xg, dyq, raw, cts, sbuf, rbuf, frow,
    s_hist, s_wv, s_fr, s_dyr, s_dyf, s_left, s_right, s_opp, s_sib, s_part, s_stat, s_misc,
):
    chunks = hist.shape[0]
    slots = hist.shape[1]
    half = xo.shape[1]
    units = chunks * LANES
    d, f = lax.axis_index("dp"), lax.axis_index("fsdp")
    hi, y = d // 4, d % 4
    lo, x, c = f // 8, (f // 2) % 4, f % 2
    oc = 1 - c
    xr, xl, xx = (x + 1) % 4, (x + 3) % 4, (x + 2) % 4

    def at(lo_, x_, c_):
        return (d, lo_ * 8 + x_ * 2 + c_)

    sibling = at(lo, x, oc)
    right, left = at(lo, xr, c), at(lo, xl, c)
    inner = at(1 - lo, x, c)
    opposite = at(lo, xx, c)
    cross = at(1 - lo, x, oc)
    flipped = (1 - lo) * 8 + x * 2 + c
    outer = ((1 - hi) * 4 + y, flipped)
    same_hi = [(hi * 4 + (y + s) % 4, f) for s in (1, 3, 2)]
    other_hi = [((1 - hi) * 4 + (y + s) % 4, flipped) for s in (0, 1, 3, 2)]
    other_hi_same_f = [((1 - hi) * 4 + (y + s) % 4, f) for s in (0, 1, 3, 2)]

    (S_XG, S_DYQ, S_XO, S_XIN, S_XIN2, S_XOUT, S_CT, S_FR, S_DYS, S_DYFS, S_W1, S_W2, S_W3, S_PS, S_XS1, S_XS2, S_XS3,
     S_CTS, S_FRS, S_ST1, S_ST2, S_ONW, S_ONN, S_OUT) = range(SEMS)

    def cols(k):
        return pl.ds(pl.multiple_of(k * LANES, LANES), LANES)

    def remote(src, dst, send, recv, to):
        pltpu.make_async_remote_copy(src, dst, send, recv, device_id=to, device_id_type=MESH).start()

    barrier = pltpu.get_barrier_semaphore()
    peers = other_hi_same_f[::-1] + other_hi[::-1] + same_hi[::-1] + [opposite, cross, inner, right, left, sibling]
    for peer in peers:
        pl.semaphore_signal(barrier, inc=1, device_id=peer, device_id_type=MESH)

    share = f // 2
    pltpu.make_async_copy(x_grad, xg, s_misc.at[S_XG]).start()
    pltpu.make_async_copy(
        dy_grad.at[:, pl.ds(pl.multiple_of(share * units, LANES), units)], dyq, s_misc.at[S_DYQ]
    ).start()

    def fetch(k):
        pltpu.make_async_copy(history.at[:, :, cols(k)], hist.at[k], s_hist.at[k]).start()
        pltpu.make_async_copy(weight.at[:, cols(k)], wv.at[k], s_wv.at[k]).start()
        pltpu.make_async_copy(fresh.at[:, cols(k)], fr.at[k], s_fr.at[k]).start()

    my_rows = pl.ds(pl.multiple_of(c * 64, 64), 64)

    def fetch_dy(k):
        column = pl.ds(pl.multiple_of(d * units + k * LANES, LANES), LANES)
        pltpu.make_async_copy(dy_grad.at[my_rows, column], dyb.at[k, d, c], s_dyr.at[k]).start()

    @pl.loop(0, chunks)
    def _(k):
        fetch_dy(k)
        fetch(k)

    pltpu.make_async_copy(x_next.at[:, pl.ds(pl.multiple_of(lo * half, LANES), half)], xo, s_misc.at[S_XO]).start()

    wait_for(xg, s_misc.at[S_XG])
    x_t = xg[...].astype(jnp.float32).T
    feature_part = jnp.sum(x_t * x_t, axis=0, keepdims=True)
    wait_for(dyq, s_misc.at[S_DYQ])
    total = jnp.zeros((LANES, LANES), jnp.float32)
    for n in range(chunks):
        piece = dyq[:, n * LANES : (n + 1) * LANES].astype(jnp.float32)
        total = total + piece * piece
    output_part = 0.5 * jnp.sum(total.T, axis=0, keepdims=True)
    row = lax.broadcasted_iota(jnp.int32, (8, LANES), 0)
    sbuf[0] = jnp.where(row == 0, feature_part, jnp.where(row == 1, output_part, 0.0))
    mine = pl.ds(pl.multiple_of(d * LANES, LANES), LANES)
    raw[:, mine] = x_t.astype(jnp.bfloat16)

    pl.semaphore_wait(barrier, len(peers))

    for r, to in enumerate((right, opposite, left)):
        remote(sbuf.at[0], rbuf.at[r], s_misc.at[S_ST1], s_stat.at[r], to)
    for to in other_hi_same_f[::-1] + same_hi[::-1]:
        remote(raw.at[:, mine], raw.at[:, mine], s_misc.at[S_CTS], s_misc.at[S_CT], to)

    def send_dy(k):
        for to in other_hi + same_hi:
            column = pl.ds(pl.multiple_of(to[0] * units + k * LANES, LANES), LANES)
            remote(dy_grad.at[my_rows, column], dyb.at[k, d, c], s_misc.at[S_DYS], s_dyr.at[k], to)

    other_half = pl.multiple_of((1 - lo) * half, LANES)
    width = half // PIECES

    def send_inner(low, high, send, recv):
        remote(
            x_next.at[low:high, pl.ds(other_half, half)], xp.at[low:high], s_misc.at[send], s_misc.at[recv], inner
        )

    def send_outer(q):
        remote(
            x_next.at[ROWS_IN:, pl.ds(pl.multiple_of(other_half + q * width, LANES), width)],
            xp.at[ROWS_IN:, pl.ds(pl.multiple_of(q * width, LANES), width)],
            s_misc.at[S_XS2], s_misc.at[S_XOUT], outer,
        )

    for r in range(3):
        wait_for(rbuf.at[r], s_stat.at[r])
    sbuf[1] = (sbuf[0] + rbuf[0]) + (rbuf[1] + rbuf[2])
    for r, to in enumerate((sibling, inner, cross)):
        remote(sbuf.at[1], rbuf.at[3 + r], s_misc.at[S_ST2], s_stat.at[3 + r], to)
    send_dy(0)
    send_inner(0, ROWS_FIRST, S_XS1, S_XIN)
    for r in range(3, 6):
        wait_for(rbuf.at[r], s_stat.at[r])
    both = (sbuf[1] + rbuf[3]) + (rbuf[4] + rbuf[5])
    frow[d] = jnp.minimum(1.0, clip_bound / jnp.sqrt(both[0:1] * both[1:2] + eps_value))
    for to in other_hi_same_f[::-1] + same_hi[::-1]:
        remote(frow.at[d], frow.at[d], s_misc.at[S_FRS], s_misc.at[S_FR], to)

    send_inner(ROWS_FIRST, ROWS_IN, S_XS3, S_XIN2)
    for k in range(1, AHEAD):
        if k <= PIECES:
            send_outer(k - 1)
        send_dy(k)

    first = newest[0]
    mixing = [band[lax.rem(first + (slots - s), slots) + 1] for s in range(slots)]
    now_coefficient = band[0]

    wait_for(raw.at[:, 0 : 7 * LANES], s_misc.at[S_CT])
    wait_for(frow.at[0:7], s_misc.at[S_FR])
    for n in range(8):
        block = slice(n * LANES, (n + 1) * LANES)
        cts[:, block] = (raw[:, block].astype(jnp.float32) * frow[n]).astype(jnp.bfloat16)

    def stage_a(k):
        wait_for(dyb.at[k, :, c], s_dyr.at[k])
        remote(dyb.at[k, :, c], dyb.at[k, :, c], s_misc.at[S_DYFS], s_dyf.at[k], sibling)

    def stage_b(k):
        wait_for(hist.at[k], s_hist.at[k])
        wait_for(wv.at[k], s_wv.at[k])
        wait_for(fr.at[k], s_fr.at[k])
        combined = mixing[0] * hist[k, 0]
        for s in range(1, slots):
            combined = combined + mixing[s] * hist[k, s]
        noise = (fr[k].astype(jnp.float32) - combined) / jnp.full(combined.shape, now_coefficient, jnp.float32)
        hist[k, 0] = noise
        wait_for(dyb.at[k, :, oc], s_dyf.at[k])
        gradient = jnp.dot(cts[...], dyb[k].reshape(8 * LANES, LANES), preferred_element_type=jnp.float32)
        updated = wv[k] - learn_rate * (gradient + (noise_multiplier * clip_bound) * noise) * (1.0 / tokens_all)
        wb[k, x, c] = updated.astype(jnp.bfloat16)
        wv[k] = updated
        block = wb.at[k, x, c]
        remote(block, block, s_misc.at[S_W1], s_left.at[k], right)
        remote(block, block, s_misc.at[S_W1], s_right.at[k], left)
        remote(block, block, s_misc.at[S_W1], s_sib.at[k], sibling)
        pltpu.make_async_copy(hist.at[k, 0], noise_now.at[:, cols(k)], s_misc.at[S_ONN]).start()
        pltpu.make_async_copy(wv.at[k], new_weight.at[:, cols(k)], s_misc.at[S_ONW]).start()

    upper, lower = pl.ds(0, LANES), pl.ds(LANES, LANES)

    def stage_c(k):
        from_left, from_right = wb.at[k, xl, c], wb.at[k, xr, c]
        wait_for(from_left, s_left.at[k])
        top = wb.at[k, xl, c, upper]
        remote(top, top, s_misc.at[S_W2], s_opp.at[k], right)
        remote(from_left, from_left, s_misc.at[S_W3], s_sib.at[k], sibling)
        wait_for(from_right, s_right.at[k])
        bottom = wb.at[k, xr, c, lower]
        remote(bottom, bottom, s_misc.at[S_W2], s_opp.at[k], left)
        remote(from_right, from_right, s_misc.at[S_W3], s_sib.at[k], sibling)

    def stage_d(k):
        block = wb.at[k, xx, c]
        wait_for(block, s_opp.at[k])
        remote(block, block, s_misc.at[S_W3], s_sib.at[k], sibling)

    def multiply(ks):
        parts = [wb[k].reshape(half, LANES) for k in ks]
        rhs = parts[0] if len(ks) == 1 else jnp.concatenate(parts, axis=1)
        theirs = jnp.dot(xp[...], rhs, preferred_element_type=jnp.float32).astype(jnp.bfloat16)
        for n, k in enumerate(ks):
            psend[k] = theirs[:, n * LANES : (n + 1) * LANES]
            remote(psend.at[k], precv.at[k], s_misc.at[S_PS], s_part.at[k], inner)
        ours = jnp.dot(xo[...], rhs, preferred_element_type=jnp.float32)
        for n, k in enumerate(ks):
            own[k] = ours[:, n * LANES : (n + 1) * LANES]

    def stage_e(k):
        @pl.when(k == 0)
        def _():
            wait_for(xo, s_misc.at[S_XO])
            wait_for(xp.at[0:ROWS_FIRST], s_misc.at[S_XIN])
            wait_for(xp.at[ROWS_FIRST:ROWS_IN], s_misc.at[S_XIN2])
            wait_for(xp.at[ROWS_IN:], s_misc.at[S_XOUT])

        wait_for(wb.at[k, :, oc], s_sib.at[k])

        @pl.when(k % 2 == 1)
        def _():
            multiply((k - 1, k))

        if chunks % 2 == 1:

            @pl.when(k == chunks - 1)
            def _():
                multiply((k,))

    def stage_f(k):
        wait_for(precv.at[k], s_part.at[k])
        obuf[k] = (own[k] + precv[k].astype(jnp.float32)).astype(jnp.bfloat16)
        pltpu.make_async_copy(obuf.at[k], next_out.at[:, cols(k)], s_misc.at[S_OUT]).start()

    def staged(stage, t, lag):
        k = t - lag

        @pl.when((k >= 0) & (k < chunks))
        def _():
            stage(k)

    @pl.loop(0, chunks + LAG_F)
    def _(t):
        staged(send_dy, t + AHEAD, 0)
        staged(stage_c, t, LAG_C)
        staged(stage_d, t, LAG_D)
        staged(stage_a, t, 0)
        staged(stage_b, t, LAG_B)
        staged(stage_e, t, LAG_E)
        staged(stage_f, t, LAG_F)

    wait_for(rbuf.at[0:3], s_misc.at[S_ST1])
    wait_for(rbuf.at[0:3], s_misc.at[S_ST2])
    wait_for(frow.at[0:7], s_misc.at[S_FRS])
    wait_for(dyb.at[:, 0:7, 0], s_misc.at[S_DYS])
    wait_for(dyb.at[:, :, 0], s_misc.at[S_DYFS])
    wait_for(xp.at[0:ROWS_FIRST], s_misc.at[S_XS1])
    wait_for(xp.at[ROWS_FIRST:ROWS_IN], s_misc.at[S_XS3])
    wait_for(xp.at[ROWS_IN:], s_misc.at[S_XS2])
    wait_for(raw.at[:, 0 : 7 * LANES], s_misc.at[S_CTS])
    wait_for(wb.at[:, 0:3, 0], s_misc.at[S_W1])
    wait_for(wb.at[:, 0, 0], s_misc.at[S_W2])
    wait_for(wb.at[:, 0:3, 0], s_misc.at[S_W3])
    wait_for(psend, s_misc.at[S_PS])
    wait_for(hist.at[:, 0], s_misc.at[S_ONN])
    wait_for(wv, s_misc.at[S_ONW])
    wait_for(obuf, s_misc.at[S_OUT])


def local(weight, history, newest, band, fresh, x_grad, dy_grad, x_next):
    slots, rows, units = history.shape
    tokens, full_width = x_next.shape
    hidden_units = dy_grad.shape[1]
    clip_bound = 2.0 * math.sqrt(full_width * hidden_units)
    tokens_all = x_grad.shape[0] * lax.axis_size("dp")
    chunks = units // LANES
    half = full_width // 2
    any_space = pl.BlockSpec(memory_space=pl.ANY)
    scalars = pl.BlockSpec(memory_space=pltpu.SMEM)
    f32, b16 = jnp.float32, jnp.bfloat16
    per_chunk = pltpu.SemaphoreType.DMA((chunks,))
    return pl.pallas_call(
        functools.partial(kernel, clip_bound, tokens_all),
        out_shape=(
            jax.ShapeDtypeStruct((rows, units), f32),
            jax.ShapeDtypeStruct((rows, units), f32),
            jax.ShapeDtypeStruct((tokens, units), b16),
        ),
        in_specs=[scalars, scalars] + [any_space] * 6,
        out_specs=(any_space,) * 3,
        scratch_shapes=[
            pltpu.VMEM((chunks, slots, rows, LANES), f32),
            pltpu.VMEM((chunks, rows, LANES), f32),
            pltpu.VMEM((chunks, rows, LANES), b16),
            pltpu.VMEM((chunks, 8, 2, 64, LANES), b16),
            pltpu.VMEM((chunks, 4, 2, rows, LANES), b16),
            pltpu.VMEM((tokens, half), b16),
            pltpu.VMEM((tokens, half), b16),
            pltpu.VMEM((chunks, tokens, LANES), b16),
            pltpu.VMEM((chunks, tokens, LANES), b16),
            pltpu.VMEM((chunks, tokens, LANES), f32),
            pltpu.VMEM((chunks, tokens, LANES), b16),
            pltpu.VMEM(x_grad.shape, b16),
            pltpu.VMEM((x_grad.shape[0], units), b16),
            pltpu.VMEM((rows, tokens_all), b16),
            pltpu.VMEM((rows, tokens_all), b16),
            pltpu.VMEM((2, 8, LANES), f32),
            pltpu.VMEM((6, 8, LANES), f32),
            pltpu.VMEM((8, 1, LANES), f32),
        ]
        + [per_chunk] * 10
        + [pltpu.SemaphoreType.DMA((6,)), pltpu.SemaphoreType.DMA((SEMS,))],
        compiler_params=pltpu.CompilerParams(
            collective_id=0, has_side_effects=True, vmem_limit_bytes=45 * 2**20
        ),
        name="step",
    )(newest, band, weight, history, fresh, x_grad, dy_grad, x_next)


def solution(mesh):
    in_specs = (
        P("fsdp", "dp"),
        P(None, "fsdp", "dp"),
        P(),
        P(),
        P("fsdp", "dp"),
        P("dp", "fsdp"),
        P("dp", None),
        P("fsdp", None),
    )
    out_specs = (P("fsdp", "dp"), P("fsdp", "dp"), P("fsdp", "dp"))
    return jax.shard_map(local, mesh=mesh, in_specs=in_specs, out_specs=out_specs, check_vma=False)
```

```python
import functools
import math

import jax
import jax.numpy as jnp
from jax import lax
from jax.experimental import pallas as pl
from jax.experimental.pallas import tpu as pltpu
from jax.sharding import PartitionSpec as P

eps_value = 1e-06
learn_rate = 0.2
noise_multiplier = 0.01

LANES = 128
ROWS_IN = 240
ROWS_FIRST = 32
SPECIAL = 4
LAG_A, LAG_B, LAG_C, LAG_D, LAG_E = 6, 10, 2, 4, 6
ROUND, RELAY, SUM, PASS, LAST = 1, 7, 13, 15, 17
SEMS = 28
MESH = pl.DeviceIdType.MESH


def wait_for(ref, sem):
    pltpu.make_async_copy(ref, ref, sem).wait()


def kernel(
    clip_bound, tokens_all,
    newest, band, weight, history, fresh, x_grad, dy_grad, x_next,
    new_weight, noise_now, next_out,
    hist, wv, fr, dyb, wb, xo, xp, psend, precv, own, obuf, xg, dyq, cts, sall, sbuf, rbuf,
    s_hist, s_wv, s_fr, s_dyr, s_dyf, s_left, s_right, s_opp, s_sib, s_part, s_stat, s_onn, s_misc,
):
    chunks = hist.shape[0]
    slots = hist.shape[1]
    half = xo.shape[1]
    units = chunks * LANES
    d, f = lax.axis_index("dp"), lax.axis_index("fsdp")
    hi, y = d // 4, d % 4
    lo, x, c = f // 8, (f // 2) % 4, f % 2
    oc = 1 - c
    xr, xl, xx = (x + 1) % 4, (x + 3) % 4, (x + 2) % 4

    def at(lo_, x_, c_):
        return (d, lo_ * 8 + x_ * 2 + c_)

    sibling = at(lo, x, oc)
    right, left = at(lo, xr, c), at(lo, xl, c)
    inner = at(1 - lo, x, c)
    opposite = at(lo, xx, c)
    cross = at(1 - lo, x, oc)
    flipped = (1 - lo) * 8 + x * 2 + c
    outer = ((1 - hi) * 4 + y, flipped)
    same_hi = [(hi * 4 + (y + s) % 4, f) for s in (1, 3, 2)]
    other_hi = [((1 - hi) * 4 + (y + s) % 4, flipped) for s in (0, 1, 3, 2)]
    d_far = (1 - hi) * 4 + y
    far = (d_far, f)

    (S_XG, S_DYQ, S_XO, S_XIN, S_XIN2, S_XOUT, S_CTY, S_CTZ, S_CTR, S_SY, S_SZ, S_SR, S_DYS, S_DYFS, S_W1, S_W2, S_W3,
     S_PS, S_XS1, S_XS2, S_XS3, S_CTS, S_CTRS, S_SS, S_SRS, S_ST, S_ONW, S_OUT) = range(SEMS)

    def cols(k):
        return pl.ds(pl.multiple_of(k * LANES, LANES), LANES)

    def remote(src, dst, send, recv, to):
        pltpu.make_async_remote_copy(src, dst, send, recv, device_id=to, device_id_type=MESH).start()

    barrier = pltpu.get_barrier_semaphore()
    peers = [far] + other_hi[::-1] + same_hi[::-1] + [opposite, cross, inner, right, left, sibling]
    for peer in peers:
        pl.semaphore_signal(barrier, inc=1, device_id=peer, device_id_type=MESH)

    share = f // 2
    pltpu.make_async_copy(x_grad, xg, s_misc.at[S_XG]).start()
    pltpu.make_async_copy(
        dy_grad.at[:, pl.ds(pl.multiple_of(share * units, LANES), units)], dyq, s_misc.at[S_DYQ]
    ).start()

    def fetch(k):
        pltpu.make_async_copy(history.at[:, :, cols(k)], hist.at[k], s_hist.at[k]).start()
        pltpu.make_async_copy(weight.at[:, cols(k)], wv.at[k], s_wv.at[k]).start()
        pltpu.make_async_copy(fresh.at[:, cols(k)], fr.at[k], s_fr.at[k]).start()

    my_rows = pl.ds(pl.multiple_of(c * 64, 64), 64)

    def fetch_dy(k):
        column = pl.ds(pl.multiple_of(d * units + k * LANES, LANES), LANES)
        pltpu.make_async_copy(dy_grad.at[my_rows, column], dyb.at[k, d, c], s_dyr.at[k]).start()

    @pl.loop(0, chunks)
    def _(k):
        fetch_dy(k)
        fetch(k)

    pltpu.make_async_copy(x_next.at[:, pl.ds(pl.multiple_of(lo * half, LANES), half)], xo, s_misc.at[S_XO]).start()

    wait_for(xg, s_misc.at[S_XG])
    x_t = xg[...].astype(jnp.float32).T
    feature_part = jnp.sum(x_t * x_t, axis=0, keepdims=True)
    wait_for(dyq, s_misc.at[S_DYQ])
    total = jnp.zeros((LANES, LANES), jnp.float32)
    for n in range(chunks):
        piece = dyq[:, n * LANES : (n + 1) * LANES].astype(jnp.float32)
        total = total + piece * piece
    output_part = 0.5 * jnp.sum(total.T, axis=0, keepdims=True)
    row = lax.broadcasted_iota(jnp.int32, (8, LANES), 0)
    sbuf[0] = jnp.where(row == 0, feature_part, jnp.where(row == 1, output_part, 0.0))
    mine = pl.ds(pl.multiple_of(d * LANES, LANES), LANES)

    pl.semaphore_wait(barrier, len(peers))

    for r, to in enumerate((right, opposite, left)):
        remote(sbuf.at[0], rbuf.at[r], s_misc.at[S_ST], s_stat.at[r], to)

    def send_dy(k):
        for to in other_hi + same_hi:
            column = pl.ds(pl.multiple_of(to[0] * units + k * LANES, LANES), LANES)
            remote(dy_grad.at[my_rows, column], dyb.at[k, d, c], s_misc.at[S_DYS], s_dyr.at[k], to)

    other_half = pl.multiple_of((1 - lo) * half, LANES)

    def send_tokens(low, high, send, recv, to):
        remote(x_next.at[low:high, pl.ds(other_half, half)], xp.at[low:high], s_misc.at[send], s_misc.at[recv], to)

    all_rows = xp.shape[0]
    send_tokens(ROWS_IN, all_rows, S_XS2, S_XOUT, outer)
    send_tokens(0, ROWS_FIRST, S_XS1, S_XIN, inner)

    first = newest[0]
    mixing = [band[lax.rem(first + (slots - s), slots) + 1] for s in range(slots)]
    now_coefficient = band[0]

    rate = learn_rate / tokens_all

    def column_of(slot):
        return slot - (slot + 15 - SPECIAL) // 16

    def slot_of(k):
        return k + (k + 16 - SPECIAL) // 16

    def second_round():
        for r in range(3):
            wait_for(rbuf.at[r], s_stat.at[r])
        sbuf[1] = (sbuf[0] + rbuf[0]) + (rbuf[1] + rbuf[2])
        for r, to in enumerate((sibling, inner, cross)):
            remote(sbuf.at[1], rbuf.at[3 + r], s_misc.at[S_ST], s_stat.at[3 + r], to)
        send_tokens(ROWS_FIRST, ROWS_IN, S_XS3, S_XIN2, inner)

    def clip_rows():
        for r in range(3, 6):
            wait_for(rbuf.at[r], s_stat.at[r])
        both = (sbuf[1] + rbuf[3]) + (rbuf[4] + rbuf[5])
        factor = jnp.minimum(1.0, clip_bound / jnp.sqrt(both[0:1] * both[1:2] + eps_value))
        clipped = (xg[...].astype(jnp.float32).T * factor).astype(jnp.bfloat16)
        cts[:, mine] = clipped
        wb[SPECIAL, x, c] = clipped
        for to in same_hi:
            remote(cts.at[:, mine], cts.at[:, mine], s_misc.at[S_CTS], s_misc.at[S_CTY], to)
        remote(cts.at[:, mine], cts.at[:, mine], s_misc.at[S_CTS], s_misc.at[S_CTZ], far)

    theirs_far = pl.ds(pl.multiple_of(d_far * LANES, LANES), LANES)

    def pass_on(ref, arrived, send, recv):
        block = ref.at[:, theirs_far]
        wait_for(block, s_misc.at[arrived])
        for to in same_hi:
            remote(block, block, s_misc.at[send], s_misc.at[recv], to)

    three = pl.ds(0, 3 * LANES)

    def stage_a(k):
        wait_for(dyb.at[k, :, c], s_dyr.at[k])
        remote(dyb.at[k, :, c], dyb.at[k, :, c], s_misc.at[S_DYFS], s_dyf.at[k], sibling)

    def stage_ring(slot):
        @pl.when(slot != SPECIAL)
        def _():
            k = column_of(slot)
            wait_for(hist.at[k], s_hist.at[k])
            wait_for(wv.at[k], s_wv.at[k])
            wait_for(fr.at[k], s_fr.at[k])
            combined = mixing[0] * hist[k, 0]
            for s in range(1, slots):
                combined = combined + mixing[s] * hist[k, s]
            noise = (fr[k].astype(jnp.float32) - combined) / jnp.full(combined.shape, now_coefficient, jnp.float32)
            hist[k, 0] = noise
            base = wv[k] - (rate * (noise_multiplier * clip_bound)) * noise
            wb[slot, x, c] = base.astype(jnp.bfloat16)
            wv[k] = base
            pltpu.make_async_copy(hist.at[k, 0], noise_now.at[:, cols(k)], s_onn).start()

        @pl.when(slot == SPECIAL)
        def _():
            clip_rows()

        block = wb.at[slot, x, c]
        remote(block, block, s_misc.at[S_W1], s_left.at[slot], right)
        remote(block, block, s_misc.at[S_W1], s_right.at[slot], left)
        remote(block, block, s_misc.at[S_W1], s_sib.at[slot], sibling)

    def stage_b(k):
        @pl.when(k == 0)
        def _():
            wait_for(cts.at[:, three], s_misc.at[S_CTY])
            wait_for(cts.at[:, three], s_misc.at[S_CTR])

        wait_for(dyb.at[k, :, oc], s_dyf.at[k])
        gradient = jnp.dot(cts[...], dyb[k].reshape(8 * LANES, LANES), preferred_element_type=jnp.float32)
        wv[k] = wv[k] - rate * gradient
        pltpu.make_async_copy(wv.at[k], new_weight.at[:, cols(k)], s_misc.at[S_ONW]).start()

    upper, lower = pl.ds(0, LANES), pl.ds(LANES, LANES)

    def stage_c(k):
        from_left, from_right = wb.at[k, xl, c], wb.at[k, xr, c]
        wait_for(from_left, s_left.at[k])
        top = wb.at[k, xl, c, upper]
        remote(top, top, s_misc.at[S_W2], s_opp.at[k], right)
        remote(from_left, from_left, s_misc.at[S_W3], s_sib.at[k], sibling)
        wait_for(from_right, s_right.at[k])
        bottom = wb.at[k, xr, c, lower]
        remote(bottom, bottom, s_misc.at[S_W2], s_opp.at[k], left)
        remote(from_right, from_right, s_misc.at[S_W3], s_sib.at[k], sibling)

    def stage_d(k):
        block = wb.at[k, xx, c]
        wait_for(block, s_opp.at[k])
        remote(block, block, s_misc.at[S_W3], s_sib.at[k], sibling)

    def multiply(ks):
        parts = [wb[k].reshape(half, LANES) for k in ks]
        rhs = parts[0] if len(ks) == 1 else jnp.concatenate(parts, axis=1)
        theirs = jnp.dot(xp[...], rhs, preferred_element_type=jnp.float32).astype(jnp.bfloat16)
        for n, k in enumerate(ks):
            psend[k] = theirs[:, n * LANES : (n + 1) * LANES]
            remote(psend.at[k], precv.at[k], s_misc.at[S_PS], s_part.at[k], inner)
        ours = jnp.dot(xo[...], rhs, preferred_element_type=jnp.float32)
        for n, k in enumerate(ks):
            own[k] = ours[:, n * LANES : (n + 1) * LANES]

    def stage_e(k):
        @pl.when(k == 0)
        def _():
            wait_for(xo, s_misc.at[S_XO])
            wait_for(xp.at[0:ROWS_FIRST], s_misc.at[S_XIN])
            wait_for(xp.at[ROWS_FIRST:ROWS_IN], s_misc.at[S_XIN2])
            wait_for(xp.at[ROWS_IN:], s_misc.at[S_XOUT])

        wait_for(wb.at[k, :, oc], s_sib.at[k])

        @pl.when(k % 2 == 1)
        def _():
            multiply((k - 1, k))

    def sum_special():
        wait_for(precv.at[SPECIAL], s_part.at[SPECIAL])
        sall[:, mine] = (own[SPECIAL] + precv[SPECIAL].astype(jnp.float32)).astype(jnp.bfloat16)
        for to in same_hi:
            remote(sall.at[:, mine], sall.at[:, mine], s_misc.at[S_SS], s_misc.at[S_SY], to)
        remote(sall.at[:, mine], sall.at[:, mine], s_misc.at[S_SS], s_misc.at[S_SZ], far)

    def stage_f(k):
        @pl.when(k == 0)
        def _():
            wait_for(sall.at[:, three], s_misc.at[S_SY])
            wait_for(sall.at[:, three], s_misc.at[S_SR])

        slot = slot_of(k)
        moved = jnp.dot(sall[...], dyb[k].reshape(8 * LANES, LANES), preferred_element_type=jnp.float32)
        wait_for(precv.at[slot], s_part.at[slot])
        obuf[k] = (own[slot] + precv[slot].astype(jnp.float32) - rate * moved).astype(jnp.bfloat16)
        pltpu.make_async_copy(obuf.at[k], next_out.at[:, cols(k)], s_misc.at[S_OUT]).start()

    ring = wb.shape[0]

    def staged(stage, k, count):
        @pl.when((k >= 0) & (k < count))
        def _():
            stage(k)

    def once(t, step, action):
        @pl.when(t == step)
        def _():
            action()

    @pl.loop(0, LAST + (chunks + 1) // 2)
    def _(t):
        once(t, ROUND, second_round)
        staged(stage_c, t - LAG_C, ring)
        staged(stage_d, t - LAG_D, ring)
        staged(stage_ring, t, ring)
        staged(send_dy, t, chunks)
        once(t, RELAY, lambda: pass_on(cts, S_CTZ, S_CTRS, S_CTR))
        once(t, SUM, sum_special)
        once(t, PASS, lambda: pass_on(sall, S_SZ, S_SRS, S_SR))
        staged(stage_e, t - LAG_E, ring)
        staged(stage_a, t - LAG_A, chunks)
        staged(stage_b, t - LAG_B, chunks)
        staged(stage_f, 2 * (t - LAST), chunks)
        staged(stage_f, 2 * (t - LAST) + 1, chunks)

    wait_for(rbuf, s_misc.at[S_ST])
    wait_for(dyb.at[:, 0:7, 0], s_misc.at[S_DYS])
    wait_for(dyb.at[:, :, 0], s_misc.at[S_DYFS])
    wait_for(xp.at[0:ROWS_FIRST], s_misc.at[S_XS1])
    wait_for(xp.at[ROWS_FIRST:ROWS_IN], s_misc.at[S_XS3])
    wait_for(xp.at[ROWS_IN:], s_misc.at[S_XS2])
    wait_for(cts.at[:, 0 : 4 * LANES], s_misc.at[S_CTS])
    wait_for(cts.at[:, three], s_misc.at[S_CTRS])
    wait_for(sall.at[:, 0 : 4 * LANES], s_misc.at[S_SS])
    wait_for(sall.at[:, three], s_misc.at[S_SRS])
    wait_for(wb.at[:, 0:3, 0], s_misc.at[S_W1])
    wait_for(wb.at[:, 0, 0], s_misc.at[S_W2])
    wait_for(wb.at[:, 0:3, 0], s_misc.at[S_W3])
    wait_for(psend, s_misc.at[S_PS])
    wait_for(hist.at[:, 0], s_onn)
    wait_for(wv, s_misc.at[S_ONW])
    wait_for(obuf, s_misc.at[S_OUT])


def local(weight, history, newest, band, fresh, x_grad, dy_grad, x_next):
    slots, rows, units = history.shape
    tokens, full_width = x_next.shape
    hidden_units = dy_grad.shape[1]
    clip_bound = 2.0 * math.sqrt(full_width * hidden_units)
    tokens_all = x_grad.shape[0] * lax.axis_size("dp")
    chunks = units // LANES
    half = full_width // 2
    any_space = pl.BlockSpec(memory_space=pl.ANY)
    scalars = pl.BlockSpec(memory_space=pltpu.SMEM)
    f32, b16 = jnp.float32, jnp.bfloat16
    per_chunk = pltpu.SemaphoreType.DMA((chunks,))
    return pl.pallas_call(
        functools.partial(kernel, clip_bound, tokens_all),
        out_shape=(
            jax.ShapeDtypeStruct((rows, units), f32),
            jax.ShapeDtypeStruct((rows, units), f32),
            jax.ShapeDtypeStruct((tokens, units), b16),
        ),
        in_specs=[scalars, scalars] + [any_space] * 6,
        out_specs=(any_space,) * 3,
        scratch_shapes=[
            pltpu.VMEM((chunks, slots, rows, LANES), f32),
            pltpu.VMEM((chunks, rows, LANES), f32),
            pltpu.VMEM((chunks, rows, LANES), b16),
            pltpu.VMEM((chunks, 8, 2, 64, LANES), b16),
            pltpu.VMEM((chunks + 1, 4, 2, rows, LANES), b16),
            pltpu.VMEM((tokens, half), b16),
            pltpu.VMEM((tokens, half), b16),
            pltpu.VMEM((chunks + 1, tokens, LANES), b16),
            pltpu.VMEM((chunks + 1, tokens, LANES), b16),
            pltpu.VMEM((chunks + 1, tokens, LANES), f32),
            pltpu.VMEM((chunks, tokens, LANES), b16),
            pltpu.VMEM(x_grad.shape, b16),
            pltpu.VMEM((x_grad.shape[0], units), b16),
            pltpu.VMEM((rows, tokens_all), b16),
            pltpu.VMEM((tokens, tokens_all), b16),
            pltpu.VMEM((2, 8, LANES), f32),
            pltpu.VMEM((6, 8, LANES), f32),
        ]
        + [per_chunk] * 5
        + [pltpu.SemaphoreType.DMA((chunks + 1,))] * 5
        + [pltpu.SemaphoreType.DMA((6,)), pltpu.SemaphoreType.DMA, pltpu.SemaphoreType.DMA((SEMS,))],
        compiler_params=pltpu.CompilerParams(
            collective_id=0, has_side_effects=True, vmem_limit_bytes=45 * 2**20
        ),
        name="step",
    )(newest, band, weight, history, fresh, x_grad, dy_grad, x_next)


def solution(mesh):
    in_specs = (
        P("fsdp", "dp"),
        P(None, "fsdp", "dp"),
        P(),
        P(),
        P("fsdp", "dp"),
        P("dp", "fsdp"),
        P("dp", None),
        P("fsdp", None),
    )
    out_specs = (P("fsdp", "dp"), P("fsdp", "dp"), P("fsdp", "dp"))
    return jax.shard_map(local, mesh=mesh, in_specs=in_specs, out_specs=out_specs, check_vma=False)
```

```python
import functools
import math

import jax
import jax.numpy as jnp
from jax import lax
from jax.experimental import pallas as pl
from jax.experimental.pallas import tpu as pltpu
from jax.sharding import PartitionSpec as P

eps_value = 1e-06
learn_rate = 0.2
noise_multiplier = 0.01

LANES = 128
ROWS_IN = 144
ROWS_SHARED = 32
ROWS_FIRST = 32
SPECIAL = 4
LAG_A, LAG_B, LAG_C, LAG_D, LAG_E = 6, 10, 2, 4, 6
SHARE = 3
ROUND, RELAY, SUM, PASS, LAST = 1, 7, 13, 16, 19
SEMS = 32
MESH = pl.DeviceIdType.MESH


def wait_for(ref, sem):
    pltpu.make_async_copy(ref, ref, sem).wait()


def kernel(
    clip_bound, tokens_all,
    newest, band, weight, history, fresh, x_grad, dy_grad, x_next,
    new_weight, noise_now, next_out,
    hist, wv, fr, dyb, wb, xo, xp, psend, precv, own, obuf, xg, dyq, cts, sall, sbuf, rbuf,
    s_hist, s_wv, s_fr, s_dyr, s_dyf, s_left, s_right, s_opp, s_sib, s_part, s_stat, s_onn, s_misc,
):
    chunks = hist.shape[0]
    slots = hist.shape[1]
    half = xo.shape[1]
    units = chunks * LANES
    d, f = lax.axis_index("dp"), lax.axis_index("fsdp")
    hi, y = d // 4, d % 4
    lo, x, c = f // 8, (f // 2) % 4, f % 2
    oc = 1 - c
    xr, xl, xx = (x + 1) % 4, (x + 3) % 4, (x + 2) % 4

    def at(lo_, x_, c_):
        return (d, lo_ * 8 + x_ * 2 + c_)

    sibling = at(lo, x, oc)
    right, left = at(lo, xr, c), at(lo, xl, c)
    inner = at(1 - lo, x, c)
    opposite = at(lo, xx, c)
    cross = at(1 - lo, x, oc)
    flipped = (1 - lo) * 8 + x * 2 + c
    outer = ((1 - hi) * 4 + y, flipped)
    same_hi = [(hi * 4 + (y + s) % 4, f) for s in (1, 3, 2)]
    other_hi = [((1 - hi) * 4 + (y + s) % 4, flipped) for s in (0, 1, 3, 2)]
    d_far = (1 - hi) * 4 + y
    far = (d_far, f)

    (S_XG, S_DYQ, S_XO, S_XIN, S_XIN2, S_XOUT, S_CTY, S_CTZ, S_CTR, S_SY, S_SZ, S_SR, S_DYS, S_DYFS, S_W1, S_W2, S_W3,
     S_PS, S_XS1, S_XS2, S_XS3, S_CTS, S_CTRS, S_SS, S_SRS, S_ST, S_ONW, S_OUT,
     S_XSH, S_XSR, S_XSS, S_XSRS) = range(SEMS)

    def cols(k):
        return pl.ds(pl.multiple_of(k * LANES, LANES), LANES)

    def remote(src, dst, send, recv, to):
        pltpu.make_async_remote_copy(src, dst, send, recv, device_id=to, device_id_type=MESH).start()

    barrier = pltpu.get_barrier_semaphore()
    peers = [far] + other_hi[::-1] + same_hi[::-1] + [opposite, cross, inner, right, left, sibling]
    for peer in peers:
        pl.semaphore_signal(barrier, inc=1, device_id=peer, device_id_type=MESH)

    share = f // 2
    pltpu.make_async_copy(x_grad, xg, s_misc.at[S_XG]).start()
    pltpu.make_async_copy(
        dy_grad.at[:, pl.ds(pl.multiple_of(share * units, LANES), units)], dyq, s_misc.at[S_DYQ]
    ).start()

    def fetch(k):
        pltpu.make_async_copy(history.at[:, :, cols(k)], hist.at[k], s_hist.at[k]).start()
        pltpu.make_async_copy(weight.at[:, cols(k)], wv.at[k], s_wv.at[k]).start()
        pltpu.make_async_copy(fresh.at[:, cols(k)], fr.at[k], s_fr.at[k]).start()

    my_rows = pl.ds(pl.multiple_of(c * 64, 64), 64)

    def fetch_dy(k):
        column = pl.ds(pl.multiple_of(d * units + k * LANES, LANES), LANES)
        pltpu.make_async_copy(dy_grad.at[my_rows, column], dyb.at[k, d, c], s_dyr.at[k]).start()

    @pl.loop(0, chunks)
    def _(k):
        fetch_dy(k)
        fetch(k)

    pltpu.make_async_copy(x_next.at[:, pl.ds(pl.multiple_of(lo * half, LANES), half)], xo, s_misc.at[S_XO]).start()

    wait_for(xg, s_misc.at[S_XG])
    x_t = xg[...].astype(jnp.float32).T
    feature_part = jnp.sum(x_t * x_t, axis=0, keepdims=True)
    wait_for(dyq, s_misc.at[S_DYQ])
    total = jnp.zeros((LANES, LANES), jnp.float32)
    for n in range(chunks):
        piece = dyq[:, n * LANES : (n + 1) * LANES].astype(jnp.float32)
        total = total + piece * piece
    output_part = 0.5 * jnp.sum(total.T, axis=0, keepdims=True)
    row = lax.broadcasted_iota(jnp.int32, (8, LANES), 0)
    sbuf[0] = jnp.where(row == 0, feature_part, jnp.where(row == 1, output_part, 0.0))
    mine = pl.ds(pl.multiple_of(d * LANES, LANES), LANES)

    pl.semaphore_wait(barrier, len(peers))

    for r, to in enumerate((right, opposite, left)):
        remote(sbuf.at[0], rbuf.at[r], s_misc.at[S_ST], s_stat.at[r], to)

    def send_dy(k):
        for to in other_hi + same_hi:
            column = pl.ds(pl.multiple_of(to[0] * units + k * LANES, LANES), LANES)
            remote(dy_grad.at[my_rows, column], dyb.at[k, d, c], s_misc.at[S_DYS], s_dyr.at[k], to)

    other_half = pl.multiple_of((1 - lo) * half, LANES)

    def send_tokens(low, high, send, recv, to):
        remote(x_next.at[low:high, pl.ds(other_half, half)], xp.at[low:high], s_misc.at[send], s_misc.at[recv], to)

    all_rows = xp.shape[0]
    rows_direct = all_rows - 4 * ROWS_SHARED
    my_share = pl.ds(pl.multiple_of(rows_direct + y * ROWS_SHARED, ROWS_SHARED), ROWS_SHARED)
    remote(
        x_next.at[my_share, pl.ds(other_half, half)], xp.at[my_share], s_misc.at[S_XSS], s_misc.at[S_XSH], outer
    )
    send_tokens(ROWS_IN, rows_direct, S_XS2, S_XOUT, outer)
    send_tokens(0, ROWS_FIRST, S_XS1, S_XIN, inner)

    first = newest[0]
    mixing = [band[lax.rem(first + (slots - s), slots) + 1] for s in range(slots)]
    now_coefficient = band[0]

    rate = learn_rate / tokens_all

    def column_of(slot):
        return slot - (slot + 15 - SPECIAL) // 16

    def slot_of(k):
        return k + (k + 16 - SPECIAL) // 16

    def second_round():
        for r in range(3):
            wait_for(rbuf.at[r], s_stat.at[r])
        sbuf[1] = (sbuf[0] + rbuf[0]) + (rbuf[1] + rbuf[2])
        for r, to in enumerate((sibling, inner, cross)):
            remote(sbuf.at[1], rbuf.at[3 + r], s_misc.at[S_ST], s_stat.at[3 + r], to)
        send_tokens(ROWS_FIRST, ROWS_IN, S_XS3, S_XIN2, inner)

    def clip_rows():
        for r in range(3, 6):
            wait_for(rbuf.at[r], s_stat.at[r])
        both = (sbuf[1] + rbuf[3]) + (rbuf[4] + rbuf[5])
        factor = jnp.minimum(1.0, clip_bound / jnp.sqrt(both[0:1] * both[1:2] + eps_value))
        clipped = (xg[...].astype(jnp.float32).T * factor).astype(jnp.bfloat16)
        cts[:, mine] = clipped
        wb[SPECIAL, x, c] = clipped
        for to in same_hi:
            remote(cts.at[:, mine], cts.at[:, mine], s_misc.at[S_CTS], s_misc.at[S_CTY], to)
        remote(cts.at[:, mine], cts.at[:, mine], s_misc.at[S_CTS], s_misc.at[S_CTZ], far)

    theirs_far = pl.ds(pl.multiple_of(d_far * LANES, LANES), LANES)

    def pass_on(ref, arrived, send, recv):
        block = ref.at[:, theirs_far]
        wait_for(block, s_misc.at[arrived])
        for to in same_hi:
            remote(block, block, s_misc.at[send], s_misc.at[recv], to)

    three = pl.ds(0, 3 * LANES)

    def share_tokens():
        block = xp.at[my_share]
        wait_for(block, s_misc.at[S_XSH])
        for to in same_hi:
            remote(block, block, s_misc.at[S_XSRS], s_misc.at[S_XSR], to)

    def stage_a(k):
        wait_for(dyb.at[k, :, c], s_dyr.at[k])
        remote(dyb.at[k, :, c], dyb.at[k, :, c], s_misc.at[S_DYFS], s_dyf.at[k], sibling)

    def stage_ring(slot):
        @pl.when(slot != SPECIAL)
        def _():
            k = column_of(slot)
            wait_for(hist.at[k], s_hist.at[k])
            wait_for(wv.at[k], s_wv.at[k])
            wait_for(fr.at[k], s_fr.at[k])
            combined = mixing[0] * hist[k, 0]
            for s in range(1, slots):
                combined = combined + mixing[s] * hist[k, s]
            noise = (fr[k].astype(jnp.float32) - combined) / jnp.full(combined.shape, now_coefficient, jnp.float32)
            hist[k, 0] = noise
            base = wv[k] - (rate * (noise_multiplier * clip_bound)) * noise
            wb[slot, x, c] = base.astype(jnp.bfloat16)
            wv[k] = base
            pltpu.make_async_copy(hist.at[k, 0], noise_now.at[:, cols(k)], s_onn).start()

        @pl.when(slot == SPECIAL)
        def _():
            clip_rows()

        block = wb.at[slot, x, c]
        remote(block, block, s_misc.at[S_W1], s_left.at[slot], right)
        remote(block, block, s_misc.at[S_W1], s_right.at[slot], left)
        remote(block, block, s_misc.at[S_W1], s_sib.at[slot], sibling)

    def stage_b(k):
        @pl.when(k == 0)
        def _():
            wait_for(cts.at[:, three], s_misc.at[S_CTY])
            wait_for(cts.at[:, three], s_misc.at[S_CTR])

        wait_for(dyb.at[k, :, oc], s_dyf.at[k])
        gradient = jnp.dot(cts[...], dyb[k].reshape(8 * LANES, LANES), preferred_element_type=jnp.float32)
        wv[k] = wv[k] - rate * gradient
        pltpu.make_async_copy(wv.at[k], new_weight.at[:, cols(k)], s_misc.at[S_ONW]).start()

    upper, lower = pl.ds(0, LANES), pl.ds(LANES, LANES)

    def stage_c(k):
        from_left, from_right = wb.at[k, xl, c], wb.at[k, xr, c]
        wait_for(from_left, s_left.at[k])
        top = wb.at[k, xl, c, upper]
        remote(top, top, s_misc.at[S_W2], s_opp.at[k], right)
        remote(from_left, from_left, s_misc.at[S_W3], s_sib.at[k], sibling)
        wait_for(from_right, s_right.at[k])
        bottom = wb.at[k, xr, c, lower]
        remote(bottom, bottom, s_misc.at[S_W2], s_opp.at[k], left)
        remote(from_right, from_right, s_misc.at[S_W3], s_sib.at[k], sibling)

    def stage_d(k):
        block = wb.at[k, xx, c]
        wait_for(block, s_opp.at[k])
        remote(block, block, s_misc.at[S_W3], s_sib.at[k], sibling)

    def multiply(ks):
        parts = [wb[k].reshape(half, LANES) for k in ks]
        rhs = parts[0] if len(ks) == 1 else jnp.concatenate(parts, axis=1)
        theirs = jnp.dot(xp[...], rhs, preferred_element_type=jnp.float32).astype(jnp.bfloat16)
        for n, k in enumerate(ks):
            psend[k] = theirs[:, n * LANES : (n + 1) * LANES]
            remote(psend.at[k], precv.at[k], s_misc.at[S_PS], s_part.at[k], inner)
        ours = jnp.dot(xo[...], rhs, preferred_element_type=jnp.float32)
        for n, k in enumerate(ks):
            own[k] = ours[:, n * LANES : (n + 1) * LANES]

    def stage_e(k):
        @pl.when(k == 0)
        def _():
            wait_for(xo, s_misc.at[S_XO])
            wait_for(xp.at[0:ROWS_FIRST], s_misc.at[S_XIN])
            wait_for(xp.at[ROWS_FIRST:ROWS_IN], s_misc.at[S_XIN2])
            wait_for(xp.at[ROWS_IN:rows_direct], s_misc.at[S_XOUT])
            wait_for(xp.at[0 : 3 * ROWS_SHARED], s_misc.at[S_XSR])

        wait_for(wb.at[k, :, oc], s_sib.at[k])

        @pl.when(k % 2 == 1)
        def _():
            multiply((k - 1, k))

    def sum_special():
        wait_for(precv.at[SPECIAL], s_part.at[SPECIAL])
        sall[:, mine] = (own[SPECIAL] + precv[SPECIAL].astype(jnp.float32)).astype(jnp.bfloat16)
        for to in same_hi:
            remote(sall.at[:, mine], sall.at[:, mine], s_misc.at[S_SS], s_misc.at[S_SY], to)
        remote(sall.at[:, mine], sall.at[:, mine], s_misc.at[S_SS], s_misc.at[S_SZ], far)

    def stage_f(k):
        @pl.when(k == 0)
        def _():
            wait_for(sall.at[:, three], s_misc.at[S_SY])
            wait_for(sall.at[:, three], s_misc.at[S_SR])

        slot = slot_of(k)
        moved = jnp.dot(sall[...], dyb[k].reshape(8 * LANES, LANES), preferred_element_type=jnp.float32)
        wait_for(precv.at[slot], s_part.at[slot])
        obuf[k] = (own[slot] + precv[slot].astype(jnp.float32) - rate * moved).astype(jnp.bfloat16)
        pltpu.make_async_copy(obuf.at[k], next_out.at[:, cols(k)], s_misc.at[S_OUT]).start()

    ring = wb.shape[0]

    def staged(stage, k, count):
        @pl.when((k >= 0) & (k < count))
        def _():
            stage(k)

    def once(t, step, action):
        @pl.when(t == step)
        def _():
            action()

    @pl.loop(0, LAST + (chunks + 1) // 2)
    def _(t):
        once(t, ROUND, second_round)
        once(t, SHARE, share_tokens)
        staged(stage_c, t - LAG_C, ring)
        staged(stage_d, t - LAG_D, ring)
        staged(stage_ring, t, ring)
        staged(send_dy, t, chunks)
        once(t, RELAY, lambda: pass_on(cts, S_CTZ, S_CTRS, S_CTR))
        once(t, SUM, sum_special)
        once(t, PASS, lambda: pass_on(sall, S_SZ, S_SRS, S_SR))
        staged(stage_e, t - LAG_E, ring)
        staged(stage_a, t - LAG_A, chunks)
        staged(stage_b, t - LAG_B, chunks)
        staged(stage_f, 2 * (t - LAST), chunks)
        staged(stage_f, 2 * (t - LAST) + 1, chunks)

    wait_for(rbuf, s_misc.at[S_ST])
    wait_for(dyb.at[:, 0:7, 0], s_misc.at[S_DYS])
    wait_for(dyb.at[:, :, 0], s_misc.at[S_DYFS])
    wait_for(xp.at[0:ROWS_FIRST], s_misc.at[S_XS1])
    wait_for(xp.at[ROWS_FIRST:ROWS_IN], s_misc.at[S_XS3])
    wait_for(xp.at[ROWS_IN:rows_direct], s_misc.at[S_XS2])
    wait_for(xp.at[0:ROWS_SHARED], s_misc.at[S_XSS])
    wait_for(xp.at[0 : 3 * ROWS_SHARED], s_misc.at[S_XSRS])
    wait_for(cts.at[:, 0 : 4 * LANES], s_misc.at[S_CTS])
    wait_for(cts.at[:, three], s_misc.at[S_CTRS])
    wait_for(sall.at[:, 0 : 4 * LANES], s_misc.at[S_SS])
    wait_for(sall.at[:, three], s_misc.at[S_SRS])
    wait_for(wb.at[:, 0:3, 0], s_misc.at[S_W1])
    wait_for(wb.at[:, 0, 0], s_misc.at[S_W2])
    wait_for(wb.at[:, 0:3, 0], s_misc.at[S_W3])
    wait_for(psend, s_misc.at[S_PS])
    wait_for(hist.at[:, 0], s_onn)
    wait_for(wv, s_misc.at[S_ONW])
    wait_for(obuf, s_misc.at[S_OUT])


def local(weight, history, newest, band, fresh, x_grad, dy_grad, x_next):
    slots, rows, units = history.shape
    tokens, full_width = x_next.shape
    hidden_units = dy_grad.shape[1]
    clip_bound = 2.0 * math.sqrt(full_width * hidden_units)
    tokens_all = x_grad.shape[0] * lax.axis_size("dp")
    chunks = units // LANES
    half = full_width // 2
    any_space = pl.BlockSpec(memory_space=pl.ANY)
    scalars = pl.BlockSpec(memory_space=pltpu.SMEM)
    f32, b16 = jnp.float32, jnp.bfloat16
    per_chunk = pltpu.SemaphoreType.DMA((chunks,))
    return pl.pallas_call(
        functools.partial(kernel, clip_bound, tokens_all),
        out_shape=(
            jax.ShapeDtypeStruct((rows, units), f32),
            jax.ShapeDtypeStruct((rows, units), f32),
            jax.ShapeDtypeStruct((tokens, units), b16),
        ),
        in_specs=[scalars, scalars] + [any_space] * 6,
        out_specs=(any_space,) * 3,
        scratch_shapes=[
            pltpu.VMEM((chunks, slots, rows, LANES), f32),
            pltpu.VMEM((chunks, rows, LANES), f32),
            pltpu.VMEM((chunks, rows, LANES), b16),
            pltpu.VMEM((chunks, 8, 2, 64, LANES), b16),
            pltpu.VMEM((chunks + 1, 4, 2, rows, LANES), b16),
            pltpu.VMEM((tokens, half), b16),
            pltpu.VMEM((tokens, half), b16),
            pltpu.VMEM((chunks + 1, tokens, LANES), b16),
            pltpu.VMEM((chunks + 1, tokens, LANES), b16),
            pltpu.VMEM((chunks + 1, tokens, LANES), f32),
            pltpu.VMEM((chunks, tokens, LANES), b16),
            pltpu.VMEM(x_grad.shape, b16),
            pltpu.VMEM((x_grad.shape[0], units), b16),
            pltpu.VMEM((rows, tokens_all), b16),
            pltpu.VMEM((tokens, tokens_all), b16),
            pltpu.VMEM((2, 8, LANES), f32),
            pltpu.VMEM((6, 8, LANES), f32),
        ]
        + [per_chunk] * 5
        + [pltpu.SemaphoreType.DMA((chunks + 1,))] * 5
        + [pltpu.SemaphoreType.DMA((6,)), pltpu.SemaphoreType.DMA, pltpu.SemaphoreType.DMA((SEMS,))],
        compiler_params=pltpu.CompilerParams(
            collective_id=0, has_side_effects=True, vmem_limit_bytes=45 * 2**20
        ),
        name="step",
    )(newest, band, weight, history, fresh, x_grad, dy_grad, x_next)


def solution(mesh):
    in_specs = (
        P("fsdp", "dp"),
        P(None, "fsdp", "dp"),
        P(),
        P(),
        P("fsdp", "dp"),
        P("dp", "fsdp"),
        P("dp", None),
        P("fsdp", None),
    )
    out_specs = (P("fsdp", "dp"), P("fsdp", "dp"), P("fsdp", "dp"))
    return jax.shard_map(local, mesh=mesh, in_specs=in_specs, out_specs=out_specs, check_vma=False)
```

```python
import functools
import math

import jax
import jax.numpy as jnp
from jax import lax
from jax.experimental import pallas as pl
from jax.experimental.pallas import tpu as pltpu
from jax.sharding import PartitionSpec as P

eps_value = 1e-06
learn_rate = 0.2
noise_multiplier = 0.01

LANES = 128
ROWS_IN = 192
ROWS_SHARED = 32
ROWS_FIRST = 32
SPECIAL = 4
LAG_A, LAG_B, LAG_C, LAG_D, LAG_E = 6, 10, 2, 4, 6
SHARE = 3
ROUND, RELAY, SUM, PASS, LAST = 1, 7, 13, 16, 19
SEMS = 32
MESH = pl.DeviceIdType.MESH


def wait_for(ref, sem):
    pltpu.make_async_copy(ref, ref, sem).wait()


def kernel(
    clip_bound, tokens_all,
    newest, band, weight, history, fresh, x_grad, dy_grad, x_next,
    new_weight, noise_now, next_out,
    hist, wv, fr, dyb, wb, xo, xp, psend, precv, own, obuf, xg, dyq, cts, sall, sbuf, rbuf,
    s_hist, s_wv, s_fr, s_dyr, s_dyf, s_left, s_right, s_opp, s_sib, s_part, s_stat, s_onn, s_misc,
):
    chunks = hist.shape[0]
    slots = hist.shape[1]
    half = xo.shape[1]
    units = chunks * LANES
    d, f = lax.axis_index("dp"), lax.axis_index("fsdp")
    hi, y = d // 4, d % 4
    lo, x, c = f // 8, (f // 2) % 4, f % 2
    oc = 1 - c
    xr, xl, xx = (x + 1) % 4, (x + 3) % 4, (x + 2) % 4

    def at(lo_, x_, c_):
        return (d, lo_ * 8 + x_ * 2 + c_)

    sibling = at(lo, x, oc)
    right, left = at(lo, xr, c), at(lo, xl, c)
    inner = at(1 - lo, x, c)
    opposite = at(lo, xx, c)
    cross = at(1 - lo, x, oc)
    flipped = (1 - lo) * 8 + x * 2 + c
    outer = ((1 - hi) * 4 + y, flipped)
    same_hi = [(hi * 4 + (y + s) % 4, f) for s in (1, 3, 2)]
    other_hi = [((1 - hi) * 4 + (y + s) % 4, flipped) for s in (0, 1, 3, 2)]
    d_far = (1 - hi) * 4 + y
    far = (d_far, f)

    (S_XG, S_DYQ, S_XO, S_XIN, S_XIN2, S_XOUT, S_CTY, S_CTZ, S_CTR, S_SY, S_SZ, S_SR, S_DYS, S_DYFS, S_W1, S_W2, S_W3,
     S_PS, S_XS1, S_XS2, S_XS3, S_CTS, S_CTRS, S_SS, S_SRS, S_ST, S_ONW, S_OUT,
     S_XSH, S_XSR, S_XSS, S_XSRS) = range(SEMS)

    def cols(k):
        return pl.ds(pl.multiple_of(k * LANES, LANES), LANES)

    def remote(src, dst, send, recv, to):
        pltpu.make_async_remote_copy(src, dst, send, recv, device_id=to, device_id_type=MESH).start()

    barrier = pltpu.get_barrier_semaphore()
    peers = [far] + other_hi[::-1] + same_hi[::-1] + [opposite, cross, inner, right, left, sibling]
    for peer in peers:
        pl.semaphore_signal(barrier, inc=1, device_id=peer, device_id_type=MESH)

    share = f // 2
    pltpu.make_async_copy(x_grad, xg, s_misc.at[S_XG]).start()
    pltpu.make_async_copy(
        dy_grad.at[:, pl.ds(pl.multiple_of(share * units, LANES), units)], dyq, s_misc.at[S_DYQ]
    ).start()

    def fetch(k):
        pltpu.make_async_copy(history.at[:, :, cols(k)], hist.at[k], s_hist.at[k]).start()
        pltpu.make_async_copy(weight.at[:, cols(k)], wv.at[k], s_wv.at[k]).start()
        pltpu.make_async_copy(fresh.at[:, cols(k)], fr.at[k], s_fr.at[k]).start()

    my_rows = pl.ds(pl.multiple_of(c * 64, 64), 64)

    def fetch_dy(k):
        column = pl.ds(pl.multiple_of(d * units + k * LANES, LANES), LANES)
        pltpu.make_async_copy(dy_grad.at[my_rows, column], dyb.at[k, d, c], s_dyr.at[k]).start()

    @pl.loop(0, chunks)
    def _(k):
        fetch_dy(k)
        fetch(k)

    pltpu.make_async_copy(x_next.at[:, pl.ds(pl.multiple_of(lo * half, LANES), half)], xo, s_misc.at[S_XO]).start()

    wait_for(xg, s_misc.at[S_XG])
    x_t = xg[...].astype(jnp.float32).T
    feature_part = jnp.sum(x_t * x_t, axis=0, keepdims=True)
    wait_for(dyq, s_misc.at[S_DYQ])
    total = jnp.zeros((LANES, LANES), jnp.float32)
    for n in range(chunks):
        piece = dyq[:, n * LANES : (n + 1) * LANES].astype(jnp.float32)
        total = total + piece * piece
    output_part = 0.5 * jnp.sum(total.T, axis=0, keepdims=True)
    row = lax.broadcasted_iota(jnp.int32, (8, LANES), 0)
    sbuf[0] = jnp.where(row == 0, feature_part, jnp.where(row == 1, output_part, 0.0))
    mine = pl.ds(pl.multiple_of(d * LANES, LANES), LANES)

    pl.semaphore_wait(barrier, len(peers))

    for r, to in enumerate((right, opposite, left)):
        remote(sbuf.at[0], rbuf.at[r], s_misc.at[S_ST], s_stat.at[r], to)

    def send_dy(k):
        for to in other_hi + same_hi:
            column = pl.ds(pl.multiple_of(to[0] * units + k * LANES, LANES), LANES)
            remote(dy_grad.at[my_rows, column], dyb.at[k, d, c], s_misc.at[S_DYS], s_dyr.at[k], to)

    other_half = pl.multiple_of((1 - lo) * half, LANES)

    def send_tokens(low, high, send, recv, to):
        remote(x_next.at[low:high, pl.ds(other_half, half)], xp.at[low:high], s_misc.at[send], s_misc.at[recv], to)

    all_rows = xp.shape[0]
    rows_direct = all_rows - 4 * ROWS_SHARED
    my_share = pl.ds(pl.multiple_of(rows_direct + y * ROWS_SHARED, ROWS_SHARED), ROWS_SHARED)
    remote(
        x_next.at[my_share, pl.ds(other_half, half)], xp.at[my_share], s_misc.at[S_XSS], s_misc.at[S_XSH], outer
    )
    send_tokens(ROWS_IN, rows_direct, S_XS2, S_XOUT, outer)
    send_tokens(0, ROWS_FIRST, S_XS1, S_XIN, inner)

    first = newest[0]
    mixing = [band[lax.rem(first + (slots - s), slots) + 1] for s in range(slots)]
    now_coefficient = band[0]

    rate = learn_rate / tokens_all

    def column_of(slot):
        return slot - (slot + 15 - SPECIAL) // 16

    def slot_of(k):
        return k + (k + 16 - SPECIAL) // 16

    def second_round():
        for r in range(3):
            wait_for(rbuf.at[r], s_stat.at[r])
        sbuf[1] = (sbuf[0] + rbuf[0]) + (rbuf[1] + rbuf[2])
        for r, to in enumerate((sibling, inner, cross)):
            remote(sbuf.at[1], rbuf.at[3 + r], s_misc.at[S_ST], s_stat.at[3 + r], to)
        send_tokens(ROWS_FIRST, ROWS_IN, S_XS3, S_XIN2, inner)

    def clip_rows():
        for r in range(3, 6):
            wait_for(rbuf.at[r], s_stat.at[r])
        both = (sbuf[1] + rbuf[3]) + (rbuf[4] + rbuf[5])
        factor = jnp.minimum(1.0, clip_bound / jnp.sqrt(both[0:1] * both[1:2] + eps_value))
        clipped = (xg[...].astype(jnp.float32).T * factor).astype(jnp.bfloat16)
        cts[:, mine] = clipped
        wb[SPECIAL, x, c] = clipped
        for to in same_hi:
            remote(cts.at[:, mine], cts.at[:, mine], s_misc.at[S_CTS], s_misc.at[S_CTY], to)
        remote(cts.at[:, mine], cts.at[:, mine], s_misc.at[S_CTS], s_misc.at[S_CTZ], far)

    theirs_far = pl.ds(pl.multiple_of(d_far * LANES, LANES), LANES)

    def pass_on(ref, arrived, send, recv):
        block = ref.at[:, theirs_far]
        wait_for(block, s_misc.at[arrived])
        for to in same_hi:
            remote(block, block, s_misc.at[send], s_misc.at[recv], to)

    three = pl.ds(0, 3 * LANES)

    def share_tokens():
        block = xp.at[my_share]
        wait_for(block, s_misc.at[S_XSH])
        for to in same_hi:
            remote(block, block, s_misc.at[S_XSRS], s_misc.at[S_XSR], to)

    def stage_a(k):
        wait_for(dyb.at[k, :, c], s_dyr.at[k])
        remote(dyb.at[k, :, c], dyb.at[k, :, c], s_misc.at[S_DYFS], s_dyf.at[k], sibling)

    def stage_ring(slot):
        @pl.when(slot != SPECIAL)
        def _():
            k = column_of(slot)
            wait_for(hist.at[k], s_hist.at[k])
            wait_for(wv.at[k], s_wv.at[k])
            wait_for(fr.at[k], s_fr.at[k])
            combined = mixing[0] * hist[k, 0]
            for s in range(1, slots):
                combined = combined + mixing[s] * hist[k, s]
            noise = (fr[k].astype(jnp.float32) - combined) / jnp.full(combined.shape, now_coefficient, jnp.float32)
            hist[k, 0] = noise
            base = wv[k] - (rate * (noise_multiplier * clip_bound)) * noise
            wb[slot, x, c] = base.astype(jnp.bfloat16)
            wv[k] = base
            pltpu.make_async_copy(hist.at[k, 0], noise_now.at[:, cols(k)], s_onn).start()

        @pl.when(slot == SPECIAL)
        def _():
            clip_rows()

        block = wb.at[slot, x, c]
        remote(block, block, s_misc.at[S_W1], s_left.at[slot], right)
        remote(block, block, s_misc.at[S_W1], s_right.at[slot], left)
        remote(block, block, s_misc.at[S_W1], s_sib.at[slot], sibling)

    def stage_b(k):
        @pl.when(k == 0)
        def _():
            wait_for(cts.at[:, three], s_misc.at[S_CTY])
            wait_for(cts.at[:, three], s_misc.at[S_CTR])

        wait_for(dyb.at[k, :, oc], s_dyf.at[k])
        gradient = jnp.dot(cts[...], dyb[k].reshape(8 * LANES, LANES), preferred_element_type=jnp.float32)
        wv[k] = wv[k] - rate * gradient
        pltpu.make_async_copy(wv.at[k], new_weight.at[:, cols(k)], s_misc.at[S_ONW]).start()

    upper, lower = pl.ds(0, LANES), pl.ds(LANES, LANES)

    def stage_c(k):
        from_left, from_right = wb.at[k, xl, c], wb.at[k, xr, c]
        wait_for(from_left, s_left.at[k])
        top = wb.at[k, xl, c, upper]
        remote(top, top, s_misc.at[S_W2], s_opp.at[k], right)
        remote(from_left, from_left, s_misc.at[S_W3], s_sib.at[k], sibling)
        wait_for(from_right, s_right.at[k])
        bottom = wb.at[k, xr, c, lower]
        remote(bottom, bottom, s_misc.at[S_W2], s_opp.at[k], left)
        remote(from_right, from_right, s_misc.at[S_W3], s_sib.at[k], sibling)

    def stage_d(k):
        block = wb.at[k, xx, c]
        wait_for(block, s_opp.at[k])
        remote(block, block, s_misc.at[S_W3], s_sib.at[k], sibling)

    def multiply(ks):
        parts = [wb[k].reshape(half, LANES) for k in ks]
        rhs = parts[0] if len(ks) == 1 else jnp.concatenate(parts, axis=1)
        theirs = jnp.dot(xp[...], rhs, preferred_element_type=jnp.float32).astype(jnp.bfloat16)
        for n, k in enumerate(ks):
            psend[k] = theirs[:, n * LANES : (n + 1) * LANES]
            remote(psend.at[k], precv.at[k], s_misc.at[S_PS], s_part.at[k], inner)
        ours = jnp.dot(xo[...], rhs, preferred_element_type=jnp.float32)
        for n, k in enumerate(ks):
            own[k] = ours[:, n * LANES : (n + 1) * LANES]

    def stage_e(k):
        @pl.when(k == 0)
        def _():
            wait_for(xo, s_misc.at[S_XO])
            wait_for(xp.at[0:ROWS_FIRST], s_misc.at[S_XIN])
            wait_for(xp.at[ROWS_FIRST:ROWS_IN], s_misc.at[S_XIN2])
            wait_for(xp.at[ROWS_IN:rows_direct], s_misc.at[S_XOUT])
            wait_for(xp.at[0 : 3 * ROWS_SHARED], s_misc.at[S_XSR])

        wait_for(wb.at[k, :, oc], s_sib.at[k])

        @pl.when(k % 2 == 1)
        def _():
            multiply((k - 1, k))

    def sum_special():
        wait_for(precv.at[SPECIAL], s_part.at[SPECIAL])
        sall[:, mine] = (own[SPECIAL] + precv[SPECIAL].astype(jnp.float32)).astype(jnp.bfloat16)
        for to in same_hi:
            remote(sall.at[:, mine], sall.at[:, mine], s_misc.at[S_SS], s_misc.at[S_SY], to)
        remote(sall.at[:, mine], sall.at[:, mine], s_misc.at[S_SS], s_misc.at[S_SZ], far)

    def stage_f(k):
        @pl.when(k == 0)
        def _():
            wait_for(sall.at[:, three], s_misc.at[S_SY])
            wait_for(sall.at[:, three], s_misc.at[S_SR])

        slot = slot_of(k)
        moved = jnp.dot(sall[...], dyb[k].reshape(8 * LANES, LANES), preferred_element_type=jnp.float32)
        wait_for(precv.at[slot], s_part.at[slot])
        obuf[k] = (own[slot] + precv[slot].astype(jnp.float32) - rate * moved).astype(jnp.bfloat16)
        pltpu.make_async_copy(obuf.at[k], next_out.at[:, cols(k)], s_misc.at[S_OUT]).start()

    ring = wb.shape[0]

    def staged(stage, k, count):
        @pl.when((k >= 0) & (k < count))
        def _():
            stage(k)

    def once(t, step, action):
        @pl.when(t == step)
        def _():
            action()

    @pl.loop(0, LAST + (chunks + 1) // 2)
    def _(t):
        once(t, ROUND, second_round)
        once(t, SHARE, share_tokens)
        staged(stage_c, t - LAG_C, ring)
        staged(stage_d, t - LAG_D, ring)
        staged(stage_ring, t, ring)
        staged(send_dy, t, chunks)
        once(t, RELAY, lambda: pass_on(cts, S_CTZ, S_CTRS, S_CTR))
        once(t, SUM, sum_special)
        once(t, PASS, lambda: pass_on(sall, S_SZ, S_SRS, S_SR))
        staged(stage_e, t - LAG_E, ring)
        staged(stage_a, t - LAG_A, chunks)
        staged(stage_b, t - LAG_B, chunks)
        staged(stage_f, 2 * (t - LAST), chunks)
        staged(stage_f, 2 * (t - LAST) + 1, chunks)

    wait_for(rbuf, s_misc.at[S_ST])
    wait_for(dyb.at[:, 0:7, 0], s_misc.at[S_DYS])
    wait_for(dyb.at[:, :, 0], s_misc.at[S_DYFS])
    wait_for(xp.at[0:ROWS_FIRST], s_misc.at[S_XS1])
    wait_for(xp.at[ROWS_FIRST:ROWS_IN], s_misc.at[S_XS3])
    wait_for(xp.at[ROWS_IN:rows_direct], s_misc.at[S_XS2])
    wait_for(xp.at[0:ROWS_SHARED], s_misc.at[S_XSS])
    wait_for(xp.at[0 : 3 * ROWS_SHARED], s_misc.at[S_XSRS])
    wait_for(cts.at[:, 0 : 4 * LANES], s_misc.at[S_CTS])
    wait_for(cts.at[:, three], s_misc.at[S_CTRS])
    wait_for(sall.at[:, 0 : 4 * LANES], s_misc.at[S_SS])
    wait_for(sall.at[:, three], s_misc.at[S_SRS])
    wait_for(wb.at[:, 0:3, 0], s_misc.at[S_W1])
    wait_for(wb.at[:, 0, 0], s_misc.at[S_W2])
    wait_for(wb.at[:, 0:3, 0], s_misc.at[S_W3])
    wait_for(psend, s_misc.at[S_PS])
    wait_for(hist.at[:, 0], s_onn)
    wait_for(wv, s_misc.at[S_ONW])
    wait_for(obuf, s_misc.at[S_OUT])


def local(weight, history, newest, band, fresh, x_grad, dy_grad, x_next):
    slots, rows, units = history.shape
    tokens, full_width = x_next.shape
    hidden_units = dy_grad.shape[1]
    clip_bound = 2.0 * math.sqrt(full_width * hidden_units)
    tokens_all = x_grad.shape[0] * lax.axis_size("dp")
    chunks = units // LANES
    half = full_width // 2
    any_space = pl.BlockSpec(memory_space=pl.ANY)
    scalars = pl.BlockSpec(memory_space=pltpu.SMEM)
    f32, b16 = jnp.float32, jnp.bfloat16
    per_chunk = pltpu.SemaphoreType.DMA((chunks,))
    return pl.pallas_call(
        functools.partial(kernel, clip_bound, tokens_all),
        out_shape=(
            jax.ShapeDtypeStruct((rows, units), f32),
            jax.ShapeDtypeStruct((rows, units), f32),
            jax.ShapeDtypeStruct((tokens, units), b16),
        ),
        in_specs=[scalars, scalars] + [any_space] * 6,
        out_specs=(any_space,) * 3,
        scratch_shapes=[
            pltpu.VMEM((chunks, slots, rows, LANES), f32),
            pltpu.VMEM((chunks, rows, LANES), f32),
            pltpu.VMEM((chunks, rows, LANES), b16),
            pltpu.VMEM((chunks, 8, 2, 64, LANES), b16),
            pltpu.VMEM((chunks + 1, 4, 2, rows, LANES), b16),
            pltpu.VMEM((tokens, half), b16),
            pltpu.VMEM((tokens, half), b16),
            pltpu.VMEM((chunks + 1, tokens, LANES), b16),
            pltpu.VMEM((chunks + 1, tokens, LANES), b16),
            pltpu.VMEM((chunks + 1, tokens, LANES), f32),
            pltpu.VMEM((chunks, tokens, LANES), b16),
            pltpu.VMEM(x_grad.shape, b16),
            pltpu.VMEM((x_grad.shape[0], units), b16),
            pltpu.VMEM((rows, tokens_all), b16),
            pltpu.VMEM((tokens, tokens_all), b16),
            pltpu.VMEM((2, 8, LANES), f32),
            pltpu.VMEM((6, 8, LANES), f32),
        ]
        + [per_chunk] * 5
        + [pltpu.SemaphoreType.DMA((chunks + 1,))] * 5
        + [pltpu.SemaphoreType.DMA((6,)), pltpu.SemaphoreType.DMA, pltpu.SemaphoreType.DMA((SEMS,))],
        compiler_params=pltpu.CompilerParams(
            collective_id=0, has_side_effects=True, vmem_limit_bytes=45 * 2**20
        ),
        name="step",
    )(newest, band, weight, history, fresh, x_grad, dy_grad, x_next)


def solution(mesh):
    in_specs = (
        P("fsdp", "dp"),
        P(None, "fsdp", "dp"),
        P(),
        P(),
        P("fsdp", "dp"),
        P("dp", "fsdp"),
        P("dp", None),
        P("fsdp", None),
    )
    out_specs = (P("fsdp", "dp"), P("fsdp", "dp"), P("fsdp", "dp"))
    return jax.shard_map(local, mesh=mesh, in_specs=in_specs, out_specs=out_specs, check_vma=False)
```
